32 devices in a mesh: grp: 2 (over y), row: 8 (over z, x), col: 2 (over core).
Axes of the slice: x: 2, y: 2, z: 4, core: 2. Of those that a mesh axis runs over, the one named last changes fastest.
Arguments:
- grad_out: bfloat16 [1024, 8192], P(('grp', 'row'), 'col'), parts along dimension 0, may hold values from -6 to 6
- hidden_act: bfloat16 [1024, 22016], P(('grp', 'col'), 'row'), parts along dimension 0, may hold values from -6 to 6
- down_weight: bfloat16 [22016, 8192], P('row', 'col'), may hold values from -0.0390625 to 0.0390625
- proj_in: bfloat16 [22016, 64], P('row'), may hold values from -0.0390625 to 0.0390625
- proj_out: bfloat16 [8192, 64], P('col'), may hold values from -0.0625 to 0.0625
- queries: bfloat16 [128, 4096], P('row', 'col'), may hold values from -0.01171875 to 0.01171875
- example_ids: int32 [1024], P(('grp', 'row')), parts along dimension 0, may hold values from 0 to 7, never falling along the last dimension, each value on 1 to 128 neighbouring positions
Outputs:
- grad_hidden: bfloat16 [1024, 22016], P(('grp', 'col'), 'row'), parts along dimension 0
- weight_grad: bfloat16 [44032, 8192], P(('grp', 'row'), 'col'), parts along dimension 0
- scores: float32 [128, 16], P(('row', 'col'), 'grp'), parts along dimension 1
The draws below stay inside these ranges and needn't reach their ends.
There are 2 independent parts, one for each index of `grp`. The reference program is written for one: setup_inputs(seed, part) draws one part's arguments, and reference() takes and returns one part's arrays. A program takes and returns all parts, laid end to end along the dimension named above; an argument that names none is the same for every part. Nothing has to cross between parts.
Inputs may be any that keep to these rules, and one draw needn't show every extreme that they name: `example_ids`: never falling along the tokens; each example holds 1 to 128 tokens, one exactly 128.
All inputs are finite; a program needn't handle non-finite values.
Results may differ from the reference program's by a relative error of at most 0.001.
Values may be sent and summed in bfloat16 or wider, within the bound.
A program may use at most 192 MiB of HBM per device.

```python
import math
import jax
import jax.numpy as jnp
import numpy as np
from jax import lax

D = 8192
FF = 22016
RANK = 64
TOK = 512
EXAMPLES = 8
MOST = 128
NQ = 128
K = 4096


def levels(stream_key, dims, cuts, least, largest):
    loudness = 1.0
    for axis_at, shards_of in cuts:
        draws = jax.random.uniform(jax.random.fold_in(jax.random.fold_in(stream_key, 6), axis_at), (shards_of,), jnp.float32, least / len(cuts), largest / len(cuts))
        loudness = loudness * jnp.repeat(jnp.exp(draws), dims[axis_at] // shards_of).reshape((-1,) + (1,) * (len(dims) - 1 - axis_at))
    return loudness


def length_profile(count, total, reach, lean):
    weights = [(1 << 20) // math.isqrt(rank ** lean) + 1 for rank in range(2, count + 1)]
    spare, counts = total - reach - (count - 1), [1] * (count - 1)
    while spare > 0:
        movable = [i for i in range(count - 1) if counts[i] < reach]
        pool, budget = sum([weights[i] for i in movable]), spare
        for i in movable:
            more = min(reach - counts[i], max(1, budget * weights[i] // pool), spare)
            counts[i] = counts[i] + more
            spare = spare - more
    return np.array([reach] + counts)


def ragged_sizes(key, amount, total, reach, slope):
    if amount == 2:
        one = jax.random.randint(key, (), max(1, total - reach), min(reach, total - 1) + 1)
        return jnp.stack([one, total - one])
    lengths = jnp.asarray(length_profile(amount, total, reach, slope), jnp.int32)
    pairs = (amount - 1) // 2
    source_of, taker = lengths[1:1 + 2 * pairs:2], lengths[2:2 + 2 * pairs:2]
    margin = jnp.minimum(source_of - 1, reach - taker)
    shifted = jax.random.randint(jax.random.fold_in(key, 1), (pairs,), 0, 1 << 20) % (margin + 1)
    lengths = lengths.at[1:1 + 2 * pairs:2].set(source_of - shifted).at[2:2 + 2 * pairs:2].set(taker + shifted)
    return lengths[jax.random.permutation(jax.random.fold_in(key, 2), amount)]


def centred(stream_key, shape, width, reach, split=(), kind=jnp.bfloat16):
    gain = levels(stream_key, shape, split, -0.22, 0.18) if split else 1.0
    result = jax.random.normal(stream_key, shape, jnp.float32) * width * gain
    return jnp.minimum(jnp.maximum(result, -reach), reach).astype(kind)


def setup_inputs(seed: int = 0, part: int = 0) -> dict:
    splits = jax.random.split(jax.random.key(seed), 8)
    own_keys = jax.random.split(jax.random.fold_in(splits[7], part), 8)
    grad_out = centred(own_keys[0], (TOK, D), 1.0, 6.0, ((0, 8), (1, 2)))
    hidden_act = centred(own_keys[1], (TOK, FF), 1.0, 6.0, ((0, 2), (1, 8)))
    down_weight = centred(splits[2], (FF, D), FF ** -0.5, 0.0390625, ((0, 8), (1, 2)))
    proj_in = centred(splits[3], (FF, RANK), FF ** -0.5, 0.0390625, ((0, 8),))
    proj_out = centred(splits[4], (D, RANK), D ** -0.5, 0.0625, ((0, 2),))
    queries = centred(splits[5], (NQ, K), (64 * K) ** -0.5, 0.01171875, ((0, 8), (1, 2)))
    example_ids = jnp.searchsorted(jnp.cumsum(ragged_sizes(own_keys[6], EXAMPLES, TOK, MOST, 1)), jnp.arange(TOK), side="right").astype(jnp.int32)
    return {"grad_out": grad_out, "hidden_act": hidden_act, "down_weight": down_weight, "proj_in": proj_in, "proj_out": proj_out, "queries": queries, "example_ids": example_ids}


def reference(grad_out, hidden_act, down_weight, proj_in, proj_out, queries, example_ids):
    grad_hidden = lax.dot_general(grad_out, down_weight, (((1,), (1,)), ((), ())), preferred_element_type=jnp.float32).astype(jnp.bfloat16)
    weight_grad = lax.dot_general(hidden_act, grad_out, (((0,), (0,)), ((), ())), preferred_element_type=jnp.float32).astype(jnp.bfloat16)
    in_factor = jnp.dot(hidden_act, proj_in, preferred_element_type=jnp.float32)
    out_factor = jnp.dot(grad_out, proj_out, preferred_element_type=jnp.float32)
    outer_terms = (in_factor[:, :, None] * out_factor[:, None, :]).reshape(in_factor.shape[0], -1)
    labels = jnp.arange(EXAMPLES, dtype=jnp.int32)
    onehot = (example_ids[None, :] == labels[:, None]).astype(jnp.float32)
    example_grad = jnp.dot(onehot, outer_terms, precision=lax.Precision.HIGHEST)
    scores = jnp.dot(queries.astype(jnp.float32), example_grad.T, precision=lax.Precision.HIGHEST)
    return (grad_hidden, weight_grad, scores)
```

```python
import functools

import jax
import jax.numpy as jnp
from jax import lax
from jax.experimental import pallas as pl
from jax.experimental.pallas import tpu as pltpu
from jax.sharding import PartitionSpec as P

EXAMPLES = 8
CHUNKS = 4
PIECES = 8
AHEAD = 2
EARLY = 6

MESH = pl.DeviceIdType.MESH
NT = (((1,), (1,)), ((), ()))


def swap(x, axis, bit):
    n = lax.axis_size(axis)
    return lax.ppermute(x, axis, [(i, i ^ bit) for i in range(n)])


def pair_order(own, other, index, axis):
    first = jnp.where(index == 0, own, other)
    second = jnp.where(index == 0, other, own)
    return jnp.concatenate([first, second], axis=axis)


def gather_rows(block):
    n = lax.axis_size("row")
    if n % 2 or n > 16:
        return lax.all_gather(block, "row", axis=0, tiled=True)
    outer = n // 2
    me = lax.axis_index("row")
    z, x = me // 2, me % 2
    held = [block]
    for k in range(1, outer):
        perm = [(i, ((i // 2 + k) % outer) * 2 + i % 2) for i in range(n)]
        held.append(lax.ppermute(block, "row", perm))
    mine = jnp.stack(held[::-1])
    theirs = swap(mine, "row", 1)
    both = pair_order(mine, theirs, x, 1)
    twice = jnp.concatenate([both, both], axis=0)
    rows = lax.dynamic_slice_in_dim(twice, outer - 1 - z, outer, 0)
    return rows.reshape((n * block.shape[0],) + block.shape[1:])


def sum_rows(x):
    n = lax.axis_size("row")
    if n & (n - 1):
        return lax.psum(x, "row")
    bit = 1
    while bit < n:
        x = x + swap(x, "row", bit)
        bit *= 2
    return x


def product_kernel(a_ref, b_ref, *refs):
    out_ref = refs[-1]
    out_ref[...] = jnp.dot(
        a_ref[...], b_ref[...], preferred_element_type=jnp.float32
    ).astype(out_ref.dtype)


def product_into(a, b, total, at, chunks):
    rows, depth = a.shape
    width = b.shape[1]
    tile = rows
    for parts in (8, 4, 2):
        if rows % (parts * 16) == 0:
            tile = rows // parts
            break
    in_specs = [
        pl.BlockSpec((tile, depth), lambda i: (i, 0)),
        pl.BlockSpec((depth, width), lambda i: (0, 0)),
    ]
    args = (a, b)
    aliases = {}
    if total is not None:
        in_specs.append(pl.BlockSpec(memory_space=pl.ANY))
        args = (a, b, total)
        aliases = {2: 0}
    return pl.pallas_call(
        product_kernel,
        grid=(rows // tile,),
        in_specs=in_specs,
        out_specs=pl.BlockSpec((tile, width), lambda i: (i, at)),
        out_shape=jax.ShapeDtypeStruct((rows, chunks * width), jnp.bfloat16),
        input_output_aliases=aliases,
        compiler_params=pltpu.CompilerParams(vmem_limit_bytes=24 << 20),
        cost_estimate=pl.CostEstimate(
            flops=2 * rows * depth * width,
            bytes_accessed=2 * (rows * depth + depth * width + rows * width),
            transcendentals=0,
        ),
    )(*args)


def plain_body(grad_out, hidden_act, down_weight, proj_in, proj_out, queries, example_ids):
    f32 = jnp.float32
    col = lax.axis_index("col")
    half_rank = proj_in.shape[1] // lax.axis_size("col")

    width = grad_out.shape[1] // CHUNKS
    parts = [
        gather_rows(lax.slice_in_dim(grad_out, c * width, (c + 1) * width, axis=1))
        for c in range(CHUNKS)
    ]

    other_hidden = swap(hidden_act, "col", 1)
    full_hidden = pair_order(hidden_act, other_hidden, col, 0)
    hidden_t = full_hidden.T

    own_proj = lax.dynamic_slice_in_dim(proj_in, col * half_rank, half_rank, 1)
    in_factor = sum_rows(
        lax.dot_general(own_proj, full_hidden, (((0,), (1,)), ((), ())), preferred_element_type=f32)
    )

    out_own = lax.dot_general(
        proj_out, grad_out, (((0,), (1,)), ((), ())), preferred_element_type=f32
    ).T
    out_own = out_own + swap(out_own, "col", 1)
    packed = gather_rows(jnp.concatenate([out_own, example_ids[:, None].astype(f32)], axis=1))
    out_factor = packed[:, :-1]
    ids = packed[:, -1].astype(jnp.int32)
    labels = jnp.arange(EXAMPLES, dtype=jnp.int32)
    onehot = ids[None, :] == labels[:, None]
    masked = jnp.where(onehot[:, None, :], in_factor[None], 0.0)
    example_grads = jnp.dot(
        masked.reshape(EXAMPLES * half_rank, -1), out_factor, precision=lax.Precision.HIGHEST
    ).reshape(EXAMPLES, -1)
    values = lax.dot_general(
        queries.astype(f32), example_grads, (((1,), (1,)), ((), ())), precision=lax.Precision.HIGHEST
    )
    share = values.shape[0] // 2
    keep = lax.dynamic_slice_in_dim(values, col * share, share, 0)
    send = lax.dynamic_slice_in_dim(values, (1 - col) * share, share, 0)
    scores = keep + swap(send, "col", 1)

    total = None
    weight_grad = None
    for c in range(CHUNKS):
        weights = lax.slice_in_dim(down_weight, c * width, (c + 1) * width, axis=1)
        term = lax.dot_general(
            parts[c], weights, (((1,), (1,)), ((), ())), preferred_element_type=f32
        )
        total = term if total is None else total + term
        weight_grad = product_into(hidden_t, parts[c], weight_grad, c, CHUNKS)
    tokens = total.shape[0] // 2
    keep = lax.dynamic_slice_in_dim(total, col * tokens, tokens, 0)
    send = lax.dynamic_slice_in_dim(total, (1 - col) * tokens, tokens, 0)
    grad_hidden = (keep + swap(send, "col", 1)).astype(jnp.bfloat16)
    return (grad_hidden, weight_grad, scores)


def gather_kernel(
    n,
    g, hto, w, pin, pout, q, ids,
    G, ht, wgp, acc, rcv, wl, wx, gx, sc,
    wbuf, gown, pin_v, pout_v, q_v, ids_v, ofo, ofx, ifp, ifx, ifs,
    pu, pd, pur, pdr, side_src, side, sidex, oft, idrow, qs, tbuf, pb, pbx,
    s_own, s_fz, s_fx, s_a, r_z, r_x, r_xo, r_a,
    t_own, t_fz, t_fx, u_z, u_x, u_xo,
    l_own, l_w, l_misc, c_send, c_recv, k_send, k_recv,
):
    f32 = jnp.float32
    pieces, tokens, width = G.shape
    rows_of = tokens // n
    ff = ht.shape[0]
    half = tokens // 2
    hw = width // 2
    nz = n // 2
    lag = nz - 1
    steps = pieces + lag
    tile = ff // 2
    hr = pin_v.shape[0]
    rank = pout_v.shape[0]
    early = wgp.shape[0]
    nq = q_v.shape[0]

    me = lax.axis_index("row")
    c = lax.axis_index("col")
    z, x = me // 2, me % 2
    has = (z < nz - 1, z > 0)
    nxt = ({"row": me + 2}, {"row": me - 2})
    xp = {"row": me + 1 - 2 * x}
    cp = {"col": 1 - c}

    def rc(src, dst, send, recv, dev):
        return pltpu.make_async_remote_copy(
            src_ref=src, dst_ref=dst, send_sem=send, recv_sem=recv, device_id=dev, device_id_type=MESH
        )

    def lc(src, dst, sem):
        return pltpu.make_async_copy(src, dst, sem)

    def rows(b):
        return pl.ds(pl.multiple_of(b * rows_of, 16), rows_of)

    def cols(s):
        return pl.ds(pl.multiple_of(s * width, 128), width)

    def at_z(d, h):
        return z - h if d == 0 else z + h

    def there(d, h):
        return z >= h if d == 0 else z + h < nz

    def own_z(d, s):
        return rc(g.at[:, cols(s)], G.at[s, rows(me)], s_own.at[d, s], r_z.at[d, 0, s], nxt[d])

    def own_x(s):
        return rc(g.at[:, cols(s)], G.at[s, rows(me)], s_own.at[2, s], r_xo.at[s], xp)

    def fwd_z(d, h, s):
        part = G.at[s, rows(at_z(d, h) * 2 + x)]
        return rc(part, part, s_fz.at[d, h - 1, s], r_z.at[d, h, s], nxt[d])

    def fwd_x(d, h, s, other=False):
        xx = 1 - x if other else x
        r = rows(at_z(d, h) * 2 + xx)
        part = G.at[s, r, pl.ds(hw, hw)] if h == 1 else G.at[s, r]
        return rc(part, part, s_fx.at[d, h - 1, s], r_x.at[d, h - 1, s], xp)

    def fwd_a(d, s):
        part = G.at[s, rows(z * 2 + 1 - x), pl.ds(0, hw)]
        return rc(part, part, s_a.at[d, s], r_a.at[d, s], nxt[d])

    def got_z(d, h, s):
        part = G.at[s, rows(at_z(d, h) * 2 + x)]
        return rc(part, part, s_own.at[d, s], r_z.at[d, h - 1, s], nxt[d])

    def got_xo(s):
        part = G.at[s, rows(z * 2 + 1 - x)]
        return rc(part, part, s_own.at[2, s], r_xo.at[s], xp)

    def got_a(d, s):
        part = G.at[s, rows(at_z(d, 1) * 2 + 1 - x), pl.ds(0, hw)]
        return rc(part, part, s_a.at[d, s], r_a.at[d, s], nxt[d])

    def t_own_z(d):
        return rc(side_src, side.at[me], t_own.at[d], u_z.at[d, 0], nxt[d])

    def t_own_x():
        return rc(side_src, side.at[me], t_own.at[2], u_xo.at[0], xp)

    def t_fwd_z(d, h):
        part = side.at[at_z(d, h) * 2 + x]
        return rc(part, part, t_fz.at[d, h - 1], u_z.at[d, h], nxt[d])

    def t_fwd_x(d, h, other=False):
        part = side.at[at_z(d, h) * 2 + (1 - x if other else x)]
        return rc(part, part, t_fx.at[d, h - 1], u_x.at[d, h - 1], xp)

    def t_got_z(d, h):
        part = side.at[at_z(d, h) * 2 + x]
        return rc(part, part, t_own.at[d], u_z.at[d, h - 1], nxt[d])

    def t_got_xo():
        part = side.at[z * 2 + 1 - x]
        return rc(part, part, t_own.at[2], u_xo.at[0], xp)

    def tok_half(ref, k):
        return ref.at[:, pl.ds(pl.multiple_of(k * half, 128), half)]

    def core_ht():
        return rc(hto, tok_half(ht, c), c_send.at[0], c_recv.at[0], cp)

    def core_wx():
        return rc(w.at[:, pl.ds((pieces - 1) * width, width)], wx, c_send.at[1], c_recv.at[1], cp)

    def core_of():
        return rc(ofo, ofx, c_send.at[2], c_recv.at[2], cp)

    def core_side():
        return rc(side, sidex, c_send.at[3], c_recv.at[3], cp)

    def core_acc():
        return rc(acc.at[1 - c], rcv, c_send.at[4], c_recv.at[4], cp)

    def core_gx():
        src = G.at[pieces - 1, pl.ds(pl.multiple_of((1 - c) * half, 16), half)]
        return rc(src, gx, c_send.at[5], c_recv.at[5], cp)

    def core_pb():
        share = nq // 2
        src = pb.at[pl.ds(pl.multiple_of((1 - c) * share, 8), share)]
        return rc(src, pbx, c_send.at[6], c_recv.at[6], cp)

    def if_x():
        return rc(ifp, ifx, k_send.at[0], k_recv.at[0], xp)

    def if_up():
        return rc(pu, pur, k_send.at[1], k_recv.at[1], nxt[0])

    def if_dn():
        return rc(pd, pdr, k_send.at[2], k_recv.at[2], nxt[1])

    def load_own(s):
        return lc(g.at[:, cols(s)], G.at[s, rows(me)], l_own.at[s])

    def load_w(s, slot):
        return lc(w.at[:, cols(s)], wbuf.at[slot], l_w.at[slot])

    loads = (
        lambda: lc(g, gown, l_misc.at[0]),
        lambda: lc(pout, pout_v, l_misc.at[1]),
        lambda: lc(hto, tok_half(ht, c), l_misc.at[2]),
        lambda: lc(pin.at[pl.ds(pl.multiple_of(c * hr, 16), hr)], pin_v, l_misc.at[3]),
        lambda: lc(q, q_v, l_misc.at[4]),
        lambda: lc(ids, ids_v, l_misc.at[5]),
        lambda: lc(w.at[:, pl.ds((pieces - 1) * width, width)], wl, l_misc.at[6]),
    )

    barrier = pltpu.get_barrier_semaphore()
    for d in (0, 1):
        @pl.when(has[d])
        def _():
            pl.semaphore_signal(barrier, inc=1, device_id=nxt[d], device_id_type=MESH)
    pl.semaphore_signal(barrier, inc=1, device_id=xp, device_id_type=MESH)
    pl.semaphore_signal(barrier, inc=1, device_id=cp, device_id_type=MESH)
    for k in (0, 1, 2, 3, 4, 5):
        loads[k]().start()
    for s in range(2):
        load_w(s, s).start()
    pl.semaphore_wait(barrier, 2 + jnp.where(has[0], 1, 0) + jnp.where(has[1], 1, 0))

    def send_own(s):
        for d in (0, 1):
            @pl.when(has[d])
            def _():
                own_z(d, s).start()
        own_x(s).start()
        load_own(s).start()

    for s in range(AHEAD):
        send_own(s)
    core_ht().start()
    core_wx().start()
    loads[6]().start()

    def hop(h, s):
        @pl.when((s >= 0) & (s < pieces))
        def _():
            for d in (0, 1):
                @pl.when(there(d, h))
                def _():
                    got_z(d, h, s).wait_recv()
                    if h < nz - 1:
                        @pl.when(has[d])
                        def _():
                            fwd_z(d, h, s).start()
                    fwd_x(d, h, s).start()

    def cross(s):
        @pl.when((s >= 0) & (s < pieces))
        def _():
            got_xo(s).wait_recv()
            for d in (0, 1):
                @pl.when(has[d])
                def _():
                    fwd_a(d, s).start()

    def finish(s):
        load_own(s).wait()
        for d in (0, 1):
            for h in range(1, nz):
                @pl.when(there(d, h))
                def _():
                    fwd_x(d, h, s, True).wait_recv()
                    if h == 1:
                        got_a(d, s).wait_recv()

    def side_hop(h, s):
        @pl.when(s == 3 + h)
        def _():
            for d in (0, 1):
                @pl.when(there(d, h))
                def _():
                    t_got_z(d, h).wait_recv()
                    if h < nz - 1:
                        @pl.when(has[d])
                        def _():
                            t_fwd_z(d, h).start()
                    t_fwd_x(d, h).start()

    def grads(s, slot, k):
        r = pl.ds(pl.multiple_of(k * tile, 16), tile)
        t = lax.dot_general(wbuf[slot, r, :], G[s], NT, preferred_element_type=f32)
        acc[0, r, :] += t[:, :half]
        acc[1, r, :] += t[:, half:]

    def weights(s, k):
        r = pl.ds(pl.multiple_of(k * tile, 16), tile)
        wgp[s, r, :] = jnp.dot(ht[r, :], G[s], preferred_element_type=f32).astype(wgp.dtype)

    def small_first(s):
        @pl.when(s == 0)
        def _():
            loads[0]().wait()
            loads[1]().wait()
            ofo[...] = lax.dot_general(pout_v[...], gown[...], NT, preferred_element_type=f32)
            pur[...] = jnp.zeros_like(pur)
            pdr[...] = jnp.zeros_like(pdr)
            side_src[...] = jnp.zeros_like(side_src)
            acc[...] = jnp.zeros_like(acc)

        @pl.when(s == 1)
        def _():
            core_of().start()
            loads[2]().wait()
            loads[3]().wait()
            core_ht().wait_recv()
            ifp[...] = jnp.dot(pin_v[...], ht[...], preferred_element_type=f32)

        @pl.when(s == 2)
        def _():
            if_x().start()
            core_of().wait_recv()
            loads[5]().wait()
            mine = pl.ds(pl.multiple_of(c * hr, 8), hr)
            both = ofo[mine, :] + ofx[mine, :]
            side_src[0:hr // 2, 0:rows_of] = both[:hr // 2]
            side_src[0:hr // 2, rows_of:2 * rows_of] = both[hr // 2:]
            side_src[hr // 2:hr // 2 + 1, 0:rows_of] = ids_v[...].astype(f32)

        @pl.when(s == 3)
        def _():
            for d in (0, 1):
                @pl.when(has[d])
                def _():
                    t_own_z(d).start()
            t_own_x().start()
            lc(side_src, side.at[me], l_misc.at[7]).start()
            if_x().wait_recv()
            ifs[...] = ifp[...] + ifx[...]

        @pl.when((s == 4 + z) & has[0])
        def _():
            @pl.when(z > 0)
            def _():
                if_up().wait_recv()
            pu[...] = ifs[...] + pur[...]

        @pl.when((s == 4 + nz - 1 - z) & has[1])
        def _():
            @pl.when(z < nz - 1)
            def _():
                if_dn().wait_recv()
            pd[...] = ifs[...] + pdr[...]

        for h in range(1, nz):
            side_hop(h, s)

        @pl.when(s == 4 + nz)
        def _():
            lc(side_src, side.at[me], l_misc.at[7]).wait()
            t_got_xo().wait_recv()
            for d in (0, 1):
                for h in range(1, nz):
                    @pl.when(there(d, h))
                    def _():
                        t_fwd_x(d, h, True).wait_recv()
            core_side().start()

            @pl.when(z == nz - 1)
            def _():
                if_up().wait_recv()

            @pl.when(z == 0)
            def _():
                if_dn().wait_recv()
            ifs[...] = ifs[...] + pur[...] + pdr[...]

        @pl.when(s == 5 + nz)
        def _():
            core_side().wait_recv()
            loads[4]().wait()
            hh = hr // 2
            mine = pl.multiple_of(c * hr, 8)
            others = pl.multiple_of((1 - c) * hr, 8)
            for b in range(n):
                t = slice(b * rows_of, (b + 1) * rows_of)
                for k in (0, 1):
                    lanes = slice(k * rows_of, (k + 1) * rows_of)
                    oft[pl.ds(mine + k * hh, hh), t] = side[b, 0:hh, lanes]
                    oft[pl.ds(others + k * hh, hh), t] = sidex[b, 0:hh, lanes]
                idrow[0:1, t] = side[b, hh:hh + 1, 0:rows_of]
            for i in range(hr):
                qs[i * nq:(i + 1) * nq, :] = q_v[:, i * rank:(i + 1) * rank].astype(f32)
            tbuf[...] = jnp.dot(
                qs[...], oft[...], preferred_element_type=f32, precision=lax.Precision.HIGHEST
            )
            per = jnp.zeros((nq, tokens), f32)
            for i in range(hr):
                per = per + tbuf[i * nq:(i + 1) * nq, :] * ifs[i:i + 1, :]
            labels = lax.broadcasted_iota(jnp.int32, (EXAMPLES, tokens), 0).astype(f32)
            mask = jnp.where(labels == idrow[...], 1.0, 0.0)
            part = lax.dot_general(
                per, mask, NT, preferred_element_type=f32, precision=lax.Precision.HIGHEST
            )
            pb[...] = jnp.zeros_like(pb)
            pb[:, 0:EXAMPLES] = part

    def small_last(s):
        @pl.when((s == 4 + z) & has[0])
        def _():
            if_up().start()

        @pl.when((s == 4 + nz - 1 - z) & has[1])
        def _():
            if_dn().start()

    def step(s, carry):
        cc = s - lag
        slot = lax.rem(jnp.maximum(cc, 0), 2)
        mid = (cc >= 0) & (cc < pieces - 1)

        @pl.when(s + AHEAD < pieces)
        def _():
            send_own(s + AHEAD)

        @pl.when(s == steps - 1)
        def _():
            core_acc().start()
            core_pb().start()

        hop(1, s)
        cross(s)

        @pl.when(mid)
        def _():
            finish(cc)
            load_w(cc, slot).wait()
            grads(cc, slot, 0)

        for h in range(2, nz):
            hop(h, s - h + 1)

        @pl.when(mid)
        def _():
            grads(cc, slot, 1)

            @pl.when(cc + 2 < pieces - 1)
            def _():
                load_w(cc + 2, slot).start()

        small_first(s)

        @pl.when((cc >= 0) & (cc < early))
        def _():
            for k in (0, 1):
                weights(cc, k)

        small_last(s)
        return carry

    lax.fori_loop(0, steps, step, 0)

    finish(pieces - 1)
    core_gx().start()

    core_wx().wait()
    loads[6]().wait()
    core_ht().wait_send()
    core_of().wait_send()
    core_side().wait_send()
    if_x().wait_send()

    def drain(s, carry):
        for d in (0, 1):
            @pl.when(has[d])
            def _():
                own_z(d, s).wait_send()
                fwd_a(d, s).wait_send()
            for h in range(1, nz):
                @pl.when(there(d, h))
                def _():
                    if h < nz - 1:
                        @pl.when(has[d])
                        def _():
                            fwd_z(d, h, s).wait_send()
                    fwd_x(d, h, s).wait_send()
        own_x(s).wait_send()
        return carry

    lax.fori_loop(0, pieces, drain, 0)
    for d in (0, 1):
        @pl.when(has[d])
        def _():
            t_own_z(d).wait_send()
            (if_up, if_dn)[d]().wait_send()
        for h in range(1, nz):
            @pl.when(there(d, h))
            def _():
                if h < nz - 1:
                    @pl.when(has[d])
                    def _():
                        t_fwd_z(d, h).wait_send()
                t_fwd_x(d, h).wait_send()
    t_own_x().wait_send()

    core_pb().wait()
    share = nq // 2
    sc[...] = pb[pl.ds(pl.multiple_of(c * share, 8), share), :] + pbx[...]
    core_acc().wait()
    core_gx().wait()


def finish_kernel(G, ht, wgp, acc, rcv, wl, wx, gx, sc, wg, gh, scores, stage, ghb, sems, gsem):
    f32 = jnp.float32
    pieces, tokens, width = G.shape
    ff = ht.shape[0]
    half = tokens // 2
    early = wgp.shape[0]
    tile = ff // 4
    c = lax.axis_index("col")

    def out(s, src):
        return pltpu.make_async_copy(src, wg.at[:, pl.ds(s * width, width)], sems.at[s])

    for s in range(early):
        out(s, wgp.at[s]).start()
    for s in range(early, pieces):
        @pl.loop(0, 4)
        def _(k):
            r = pl.ds(pl.multiple_of(k * tile, 16), tile)
            stage[s - early, r, :] = jnp.dot(
                ht[r, :], G[s], preferred_element_type=f32
            ).astype(stage.dtype)
        out(s, stage.at[s - early]).start()
    mine = pl.ds(pl.multiple_of(c * half, 16), half)

    @pl.loop(0, 4)
    def _(k):
        r = pl.ds(pl.multiple_of(k * tile, 16), tile)
        t = acc[c, r, :] + rcv[r, :]
        t = t + lax.dot_general(wl[r, :], G[pieces - 1, mine, :], NT, preferred_element_type=f32)
        t = t + lax.dot_general(wx[r, :], gx[...], NT, preferred_element_type=f32)
        ghb[r, :] = t.astype(ghb.dtype)
        pltpu.make_async_copy(ghb.at[r], gh.at[r], gsem.at[k]).start()
    scores[...] = sc[:, 0:scores.shape[1]]
    for k in range(4):
        r = pl.ds(k * tile, tile)
        pltpu.make_async_copy(ghb.at[r], gh.at[r], gsem.at[k]).wait()
    for s in range(pieces):
        out(s, wgp.at[s] if s < early else stage.at[s - early]).wait()


def fused_body(grad_out, hidden_act, down_weight, proj_in, proj_out, queries, example_ids):
    bf16, f32, dma = jnp.bfloat16, jnp.float32, pltpu.SemaphoreType.DMA
    n = lax.axis_size("row")
    nz = n // 2
    rows_of, depth = grad_out.shape
    tokens = n * rows_of
    half, ff = hidden_act.shape
    width = depth // PIECES
    rank = proj_in.shape[1]
    hr = rank // 2
    nq = queries.shape[0]
    vm = pltpu.VMEM
    v_spec = pl.BlockSpec(memory_space=pltpu.VMEM)
    h_spec = pl.BlockSpec(memory_space=pltpu.HBM)

    args = (
        grad_out, hidden_act.T, down_weight, proj_in.T, proj_out.T, queries, example_ids.reshape(1, -1)
    )
    args = tuple(pltpu.with_memory_space_constraint(a, pltpu.HBM) for a in args)
    held = pl.pallas_call(
        functools.partial(gather_kernel, n),
        in_specs=[h_spec] * 7,
        out_specs=(v_spec,) * 9,
        out_shape=(
            vm((PIECES, tokens, width), bf16),
            vm((ff, tokens), bf16),
            vm((EARLY, ff, width), bf16),
            vm((2, ff, half), f32),
            vm((ff, half), f32),
            vm((ff, width), bf16),
            vm((ff, width), bf16),
            vm((half, width), bf16),
            vm((nq // 2, 128), f32),
        ),
        scratch_shapes=[
            vm((2, ff, width), bf16),
            vm((rows_of, depth), bf16),
            vm((hr, ff), bf16),
            vm((rank, depth), bf16),
            vm((nq, hr * rank), bf16),
            vm((1, rows_of), jnp.int32),
            vm((rank, rows_of), f32),
            vm((rank, rows_of), f32),
        ] + [vm((hr, tokens), f32)] * 7 + [
            vm((hr // 2 + 8, 2 * rows_of), f32),
            vm((n, hr // 2 + 8, 2 * rows_of), f32),
            vm((n, hr // 2 + 8, 2 * rows_of), f32),
            vm((rank, tokens), f32),
            vm((1, tokens), f32),
            vm((hr * nq, rank), f32),
            vm((hr * nq, tokens), f32),
            vm((nq, 128), f32),
            vm((nq // 2, 128), f32),
            dma((3, PIECES)),
            dma((2, nz - 2, PIECES)),
            dma((2, nz - 1, PIECES)),
            dma((2, PIECES)),
            dma((2, nz - 1, PIECES)),
            dma((2, nz - 1, PIECES)),
            dma((PIECES,)),
            dma((2, PIECES)),
            dma((3,)),
            dma((2, nz - 2)),
            dma((2, nz - 1)),
            dma((2, nz - 1)),
            dma((2, nz - 1)),
            dma((1,)),
            dma((PIECES,)),
            dma((2,)),
            dma((8,)),
            dma((7,)),
            dma((7,)),
            dma((3,)),
            dma((3,)),
        ],
        compiler_params=pltpu.CompilerParams(
            collective_id=0, has_side_effects=True, vmem_limit_bytes=12 << 20
        ),
    )(*args)

    wg, gh, scores = pl.pallas_call(
        finish_kernel,
        in_specs=[v_spec] * 9,
        out_specs=(h_spec, h_spec, v_spec),
        out_shape=(
            jax.ShapeDtypeStruct((ff, depth), bf16),
            jax.ShapeDtypeStruct((ff, half), bf16),
            jax.ShapeDtypeStruct((nq // 2, EXAMPLES), f32),
        ),
        scratch_shapes=[
            vm((PIECES - EARLY, ff, width), bf16),
            vm((ff, half), bf16),
            dma((PIECES,)),
            dma((4,)),
        ],
        compiler_params=pltpu.CompilerParams(vmem_limit_bytes=12 << 20),
    )(*held)
    return (gh.T, wg, scores)


def fits(mesh, shapes):
    n = mesh.shape["row"]
    if mesh.shape["col"] != 2 or n % 2 or not 6 <= n <= 16 or PIECES < n // 2 + 4:
        return False
    grad_out, hidden_act, _, proj_in, _, queries, _ = shapes
    parts = mesh.shape["grp"]
    rows_of = grad_out[0] // (parts * n)
    ff = hidden_act[1] // n
    rank = proj_in[1]
    return (
        2 * rows_of == 128
        and grad_out[1] % (2 * PIECES * 256) == 0
        and ff % 64 == 0
        and rank % 32 == 0
        and queries[0] % (16 * n) == 0
        and queries[1] == rank * rank
        and ff * (rows_of * n + grad_out[1]) < 24 << 20
    )


def solution(mesh):
    def run(*args):
        body = fused_body if fits(mesh, [a.shape for a in args]) else plain_body
        return jax.shard_map(
            body,
            mesh=mesh,
            in_specs=(
                P(("grp", "row"), "col"),
                P(("grp", "col"), "row"),
                P("row", "col"),
                P("row", None),
                P("col", None),
                P("row", "col"),
                P(("grp", "row")),
            ),
            out_specs=(P(("grp", "col"), "row"), P(("grp", "row"), "col"), P(("row", "col"), "grp")),
            check_vma=False,
        )(*args)

    return run
```

```python
import functools

import jax
import jax.numpy as jnp
from jax import lax
from jax.experimental import pallas as pl
from jax.experimental.pallas import tpu as pltpu
from jax.sharding import PartitionSpec as P

EXAMPLES = 8
CHUNKS = 4
PIECES = 8
AHEAD = 2
EARLY = 5

MESH = pl.DeviceIdType.MESH
NT = (((1,), (1,)), ((), ()))


def swap(x, axis, bit):
    n = lax.axis_size(axis)
    return lax.ppermute(x, axis, [(i, i ^ bit) for i in range(n)])


def pair_order(own, other, index, axis):
    first = jnp.where(index == 0, own, other)
    second = jnp.where(index == 0, other, own)
    return jnp.concatenate([first, second], axis=axis)


def gather_rows(block):
    n = lax.axis_size("row")
    if n % 2 or n > 16:
        return lax.all_gather(block, "row", axis=0, tiled=True)
    outer = n // 2
    me = lax.axis_index("row")
    z, x = me // 2, me % 2
    held = [block]
    for k in range(1, outer):
        perm = [(i, ((i // 2 + k) % outer) * 2 + i % 2) for i in range(n)]
        held.append(lax.ppermute(block, "row", perm))
    mine = jnp.stack(held[::-1])
    theirs = swap(mine, "row", 1)
    both = pair_order(mine, theirs, x, 1)
    twice = jnp.concatenate([both, both], axis=0)
    rows = lax.dynamic_slice_in_dim(twice, outer - 1 - z, outer, 0)
    return rows.reshape((n * block.shape[0],) + block.shape[1:])


def sum_rows(x):
    n = lax.axis_size("row")
    if n & (n - 1):
        return lax.psum(x, "row")
    bit = 1
    while bit < n:
        x = x + swap(x, "row", bit)
        bit *= 2
    return x


def product_kernel(a_ref, b_ref, *refs):
    out_ref = refs[-1]
    out_ref[...] = jnp.dot(
        a_ref[...], b_ref[...], preferred_element_type=jnp.float32
    ).astype(out_ref.dtype)


def product_into(a, b, total, at, chunks):
    rows, depth = a.shape
    width = b.shape[1]
    tile = rows
    for parts in (8, 4, 2):
        if rows % (parts * 16) == 0:
            tile = rows // parts
            break
    in_specs = [
        pl.BlockSpec((tile, depth), lambda i: (i, 0)),
        pl.BlockSpec((depth, width), lambda i: (0, 0)),
    ]
    args = (a, b)
    aliases = {}
    if total is not None:
        in_specs.append(pl.BlockSpec(memory_space=pl.ANY))
        args = (a, b, total)
        aliases = {2: 0}
    return pl.pallas_call(
        product_kernel,
        grid=(rows // tile,),
        in_specs=in_specs,
        out_specs=pl.BlockSpec((tile, width), lambda i: (i, at)),
        out_shape=jax.ShapeDtypeStruct((rows, chunks * width), jnp.bfloat16),
        input_output_aliases=aliases,
        compiler_params=pltpu.CompilerParams(vmem_limit_bytes=24 << 20),
        cost_estimate=pl.CostEstimate(
            flops=2 * rows * depth * width,
            bytes_accessed=2 * (rows * depth + depth * width + rows * width),
            transcendentals=0,
        ),
    )(*args)


def plain_body(grad_out, hidden_act, down_weight, proj_in, proj_out, queries, example_ids):
    f32 = jnp.float32
    col = lax.axis_index("col")
    half_rank = proj_in.shape[1] // lax.axis_size("col")

    width = grad_out.shape[1] // CHUNKS
    parts = [
        gather_rows(lax.slice_in_dim(grad_out, c * width, (c + 1) * width, axis=1))
        for c in range(CHUNKS)
    ]

    other_hidden = swap(hidden_act, "col", 1)
    full_hidden = pair_order(hidden_act, other_hidden, col, 0)
    hidden_t = full_hidden.T

    own_proj = lax.dynamic_slice_in_dim(proj_in, col * half_rank, half_rank, 1)
    in_factor = sum_rows(
        lax.dot_general(own_proj, full_hidden, (((0,), (1,)), ((), ())), preferred_element_type=f32)
    )

    out_own = lax.dot_general(
        proj_out, grad_out, (((0,), (1,)), ((), ())), preferred_element_type=f32
    ).T
    out_own = out_own + swap(out_own, "col", 1)
    packed = gather_rows(jnp.concatenate([out_own, example_ids[:, None].astype(f32)], axis=1))
    out_factor = packed[:, :-1]
    ids = packed[:, -1].astype(jnp.int32)
    labels = jnp.arange(EXAMPLES, dtype=jnp.int32)
    onehot = ids[None, :] == labels[:, None]
    masked = jnp.where(onehot[:, None, :], in_factor[None], 0.0)
    example_grads = jnp.dot(
        masked.reshape(EXAMPLES * half_rank, -1), out_factor, precision=lax.Precision.HIGHEST
    ).reshape(EXAMPLES, -1)
    values = lax.dot_general(
        queries.astype(f32), example_grads, (((1,), (1,)), ((), ())), precision=lax.Precision.HIGHEST
    )
    share = values.shape[0] // 2
    keep = lax.dynamic_slice_in_dim(values, col * share, share, 0)
    send = lax.dynamic_slice_in_dim(values, (1 - col) * share, share, 0)
    scores = keep + swap(send, "col", 1)

    total = None
    weight_grad = None
    for c in range(CHUNKS):
        weights = lax.slice_in_dim(down_weight, c * width, (c + 1) * width, axis=1)
        term = lax.dot_general(
            parts[c], weights, (((1,), (1,)), ((), ())), preferred_element_type=f32
        )
        total = term if total is None else total + term
        weight_grad = product_into(hidden_t, parts[c], weight_grad, c, CHUNKS)
    tokens = total.shape[0] // 2
    keep = lax.dynamic_slice_in_dim(total, col * tokens, tokens, 0)
    send = lax.dynamic_slice_in_dim(total, (1 - col) * tokens, tokens, 0)
    grad_hidden = (keep + swap(send, "col", 1)).astype(jnp.bfloat16)
    return (grad_hidden, weight_grad, scores)


def gather_kernel(
    n,
    g, hto, w, pin, pout, q, ids,
    G, ht, wgp, acc, rcv, wl, wx, gx, sc,
    wbuf, gown, pin_v, pout_v, q_v, ids_v, ofo, ofx, ifp, ifx, ifs,
    pu, pd, pur, pdr, side_src, side, sidex, oft, idrow, qs, tbuf, pb, pbx,
    s_own, s_fz, s_fx, s_a, r_z, r_x, r_xo, r_a,
    t_own, t_fz, t_fx, u_z, u_x, u_xo,
    l_own, l_w, l_misc, c_send, c_recv, k_send, k_recv,
):
    f32 = jnp.float32
    pieces, tokens, width = G.shape
    rows_of = tokens // n
    ff = ht.shape[0]
    half = tokens // 2
    quarter = width // 4
    nz = n // 2
    lag = nz - 1
    steps = pieces + lag - 1
    tile = ff // 2
    hr = pin_v.shape[0]
    rank = pout_v.shape[0]
    early = wgp.shape[0]
    nq = q_v.shape[0]

    me = lax.axis_index("row")
    c = lax.axis_index("col")
    z, x = me // 2, me % 2
    has = (z < nz - 1, z > 0)
    nxt = ({"row": me + 2}, {"row": me - 2})
    xp = {"row": me + 1 - 2 * x}
    cp = {"col": 1 - c}

    def rc(src, dst, send, recv, dev):
        return pltpu.make_async_remote_copy(
            src_ref=src, dst_ref=dst, send_sem=send, recv_sem=recv, device_id=dev, device_id_type=MESH
        )

    def lc(src, dst, sem):
        return pltpu.make_async_copy(src, dst, sem)

    def rows(b):
        return pl.ds(pl.multiple_of(b * rows_of, 16), rows_of)

    def cols(s):
        return pl.ds(pl.multiple_of(s * width, 128), width)

    def at_z(d, h):
        return z - h if d == 0 else z + h

    def there(d, h):
        return z >= h if d == 0 else z + h < nz

    def own_z(d, s):
        return rc(g.at[:, cols(s)], G.at[s, rows(me)], s_own.at[d, s], r_z.at[d, 0, s], nxt[d])

    def own_x(s):
        return rc(g.at[:, cols(s)], G.at[s, rows(me)], s_own.at[2, s], r_xo.at[s], xp)

    def fwd_z(d, h, s):
        part = G.at[s, rows(at_z(d, h) * 2 + x)]
        return rc(part, part, s_fz.at[d, h - 1, s], r_z.at[d, h, s], nxt[d])

    def fwd_x(d, h, s, odd, other=False):
        xx = 1 - x if other else x
        r = rows(at_z(d, h) * 2 + xx)
        cut = quarter * (1 + odd)
        part = G.at[s, r, pl.ds(cut, width - cut)] if h == 1 else G.at[s, r]
        return rc(part, part, s_fx.at[d, h - 1, s], r_x.at[d, h - 1, s], xp)

    def fwd_a(d, s, odd):
        part = G.at[s, rows(z * 2 + 1 - x), pl.ds(0, quarter * (1 + odd))]
        return rc(part, part, s_a.at[d, s], r_a.at[d, s], nxt[d])

    def by_parity(s, f):
        for odd in (0, 1):
            @pl.when(lax.rem(s, 2) == odd)
            def _():
                f(odd)

    def got_z(d, h, s):
        part = G.at[s, rows(at_z(d, h) * 2 + x)]
        return rc(part, part, s_own.at[d, s], r_z.at[d, h - 1, s], nxt[d])

    def got_xo(s):
        part = G.at[s, rows(z * 2 + 1 - x)]
        return rc(part, part, s_own.at[2, s], r_xo.at[s], xp)

    def got_a(d, s, odd):
        part = G.at[s, rows(at_z(d, 1) * 2 + 1 - x), pl.ds(0, quarter * (1 + odd))]
        return rc(part, part, s_a.at[d, s], r_a.at[d, s], nxt[d])

    def t_own_z(d):
        return rc(side_src, side.at[me], t_own.at[d], u_z.at[d, 0], nxt[d])

    def t_own_x():
        return rc(side_src, side.at[me], t_own.at[2], u_xo.at[0], xp)

    def t_fwd_z(d, h):
        part = side.at[at_z(d, h) * 2 + x]
        return rc(part, part, t_fz.at[d, h - 1], u_z.at[d, h], nxt[d])

    def t_fwd_x(d, h, other=False):
        part = side.at[at_z(d, h) * 2 + (1 - x if other else x)]
        return rc(part, part, t_fx.at[d, h - 1], u_x.at[d, h - 1], xp)

    def t_got_z(d, h):
        part = side.at[at_z(d, h) * 2 + x]
        return rc(part, part, t_own.at[d], u_z.at[d, h - 1], nxt[d])

    def t_got_xo():
        part = side.at[z * 2 + 1 - x]
        return rc(part, part, t_own.at[2], u_xo.at[0], xp)

    def tok_half(ref, k):
        return ref.at[:, pl.ds(pl.multiple_of(k * half, 128), half)]

    def core_ht():
        return rc(hto, tok_half(ht, c), c_send.at[0], c_recv.at[0], cp)

    def core_wx():
        return rc(w.at[:, pl.ds((pieces - 1) * width, width)], wx, c_send.at[1], c_recv.at[1], cp)

    def core_of():
        return rc(ofo, ofx, c_send.at[2], c_recv.at[2], cp)

    def core_side():
        return rc(side, sidex, c_send.at[3], c_recv.at[3], cp)

    def core_acc(k):
        r = pl.ds(k * tile, tile)
        return rc(acc.at[1 - c, r], rcv.at[r], k_send.at[3 + k], k_recv.at[3 + k], cp)

    def core_gx():
        src = G.at[pieces - 1, pl.ds(pl.multiple_of((1 - c) * half, 16), half)]
        return rc(src, gx, c_send.at[5], c_recv.at[5], cp)

    def core_pb():
        share = nq // 2
        src = pb.at[pl.ds(pl.multiple_of((1 - c) * share, 8), share)]
        return rc(src, pbx, c_send.at[6], c_recv.at[6], cp)

    def if_x():
        return rc(ifp, ifx, k_send.at[0], k_recv.at[0], xp)

    def if_up():
        return rc(pu, pur, k_send.at[1], k_recv.at[1], nxt[0])

    def if_dn():
        return rc(pd, pdr, k_send.at[2], k_recv.at[2], nxt[1])

    def load_own(s):
        return lc(g.at[:, cols(s)], G.at[s, rows(me)], l_own.at[s])

    def load_w(s, slot):
        return lc(w.at[:, cols(s)], wbuf.at[slot], l_w.at[slot])

    loads = (
        lambda: lc(g, gown, l_misc.at[0]),
        lambda: lc(pout, pout_v, l_misc.at[1]),
        lambda: lc(hto, tok_half(ht, c), l_misc.at[2]),
        lambda: lc(pin.at[pl.ds(pl.multiple_of(c * hr, 16), hr)], pin_v, l_misc.at[3]),
        lambda: lc(q, q_v, l_misc.at[4]),
        lambda: lc(ids, ids_v, l_misc.at[5]),
        lambda: lc(w.at[:, pl.ds((pieces - 1) * width, width)], wl, l_misc.at[6]),
    )

    barrier = pltpu.get_barrier_semaphore()
    for d in (0, 1):
        @pl.when(has[d])
        def _():
            pl.semaphore_signal(barrier, inc=1, device_id=nxt[d], device_id_type=MESH)
    pl.semaphore_signal(barrier, inc=1, device_id=xp, device_id_type=MESH)
    pl.semaphore_signal(barrier, inc=1, device_id=cp, device_id_type=MESH)
    for k in (0, 1, 2, 3, 4, 5):
        loads[k]().start()
    for s in range(2):
        load_w(s, s).start()
    pl.semaphore_wait(barrier, 2 + jnp.where(has[0], 1, 0) + jnp.where(has[1], 1, 0))

    def send_own(s):
        for d in (0, 1):
            @pl.when(has[d])
            def _():
                own_z(d, s).start()
        own_x(s).start()
        load_own(s).start()

    for s in range(AHEAD):
        send_own(s)
    core_ht().start()
    core_wx().start()
    loads[6]().start()

    def hop(h, s):
        @pl.when((s >= 0) & (s < pieces))
        def _():
            for d in (0, 1):
                @pl.when(there(d, h))
                def _():
                    got_z(d, h, s).wait_recv()
                    if h < nz - 1:
                        @pl.when(has[d])
                        def _():
                            fwd_z(d, h, s).start()
                    if h == 1:
                        by_parity(s, lambda odd: fwd_x(d, h, s, odd).start())
                    else:
                        fwd_x(d, h, s, 0).start()

    def cross(s):
        @pl.when((s >= 0) & (s < pieces))
        def _():
            got_xo(s).wait_recv()
            for d in (0, 1):
                @pl.when(has[d])
                def _():
                    by_parity(s, lambda odd: fwd_a(d, s, odd).start())

    def finish(s):
        load_own(s).wait()
        for d in (0, 1):
            for h in range(1, nz):
                @pl.when(there(d, h))
                def _():
                    if h == 1:
                        def both(odd):
                            fwd_x(d, h, s, odd, True).wait_recv()
                            got_a(d, s, odd).wait_recv()

                        by_parity(s, both)
                    else:
                        fwd_x(d, h, s, 0, True).wait_recv()

    def side_hop(h, s):
        @pl.when(s == 3 + h)
        def _():
            for d in (0, 1):
                @pl.when(there(d, h))
                def _():
                    t_got_z(d, h).wait_recv()
                    if h < nz - 1:
                        @pl.when(has[d])
                        def _():
                            t_fwd_z(d, h).start()
                    t_fwd_x(d, h).start()

    def grads(s, slot, k):
        r = pl.ds(pl.multiple_of(k * tile, 16), tile)
        t = lax.dot_general(wbuf[slot, r, :], G[s], NT, preferred_element_type=f32)
        acc[0, r, :] += t[:, :half]
        acc[1, r, :] += t[:, half:]

    def weights(s, k):
        r = pl.ds(pl.multiple_of(k * tile, 16), tile)
        wgp[s, r, :] = jnp.dot(ht[r, :], G[s], preferred_element_type=f32).astype(wgp.dtype)

    def small_first(s):
        @pl.when(s == 0)
        def _():
            loads[0]().wait()
            loads[1]().wait()
            ofo[...] = lax.dot_general(pout_v[...], gown[...], NT, preferred_element_type=f32)
            pur[...] = jnp.zeros_like(pur)
            pdr[...] = jnp.zeros_like(pdr)
            side_src[...] = jnp.zeros_like(side_src)
            acc[...] = jnp.zeros_like(acc)

        @pl.when(s == 1)
        def _():
            core_of().start()
            loads[2]().wait()
            loads[3]().wait()
            core_ht().wait_recv()
            ifp[...] = jnp.dot(pin_v[...], ht[...], preferred_element_type=f32)

        @pl.when(s == 2)
        def _():
            if_x().start()
            core_of().wait_recv()
            loads[5]().wait()
            mine = pl.ds(pl.multiple_of(c * hr, 8), hr)
            both = ofo[mine, :] + ofx[mine, :]
            side_src[0:hr // 2, 0:rows_of] = both[:hr // 2]
            side_src[0:hr // 2, rows_of:2 * rows_of] = both[hr // 2:]
            side_src[hr // 2:hr // 2 + 1, 0:rows_of] = ids_v[...].astype(f32)

        @pl.when(s == 3)
        def _():
            for d in (0, 1):
                @pl.when(has[d])
                def _():
                    t_own_z(d).start()
            t_own_x().start()
            lc(side_src, side.at[me], l_misc.at[7]).start()
            if_x().wait_recv()
            ifs[...] = ifp[...] + ifx[...]

        @pl.when((s == 4 + z) & has[0])
        def _():
            @pl.when(z > 0)
            def _():
                if_up().wait_recv()
            pu[...] = ifs[...] + pur[...]

        @pl.when((s == 4 + nz - 1 - z) & has[1])
        def _():
            @pl.when(z < nz - 1)
            def _():
                if_dn().wait_recv()
            pd[...] = ifs[...] + pdr[...]

        for h in range(1, nz):
            side_hop(h, s)

        @pl.when(s == 4 + nz)
        def _():
            lc(side_src, side.at[me], l_misc.at[7]).wait()
            t_got_xo().wait_recv()
            for d in (0, 1):
                for h in range(1, nz):
                    @pl.when(there(d, h))
                    def _():
                        t_fwd_x(d, h, True).wait_recv()
            core_side().start()

            @pl.when(z == nz - 1)
            def _():
                if_up().wait_recv()

            @pl.when(z == 0)
            def _():
                if_dn().wait_recv()
            ifs[...] = ifs[...] + pur[...] + pdr[...]

        @pl.when(s == 5 + nz)
        def _():
            core_side().wait_recv()
            loads[4]().wait()
            hh = hr // 2
            mine = pl.multiple_of(c * hr, 8)
            others = pl.multiple_of((1 - c) * hr, 8)
            for b in range(n):
                t = slice(b * rows_of, (b + 1) * rows_of)
                for k in (0, 1):
                    lanes = slice(k * rows_of, (k + 1) * rows_of)
                    oft[pl.ds(mine + k * hh, hh), t] = side[b, 0:hh, lanes]
                    oft[pl.ds(others + k * hh, hh), t] = sidex[b, 0:hh, lanes]
                idrow[0:1, t] = side[b, hh:hh + 1, 0:rows_of]
            for i in range(hr):
                qs[i * nq:(i + 1) * nq, :] = q_v[:, i * rank:(i + 1) * rank].astype(f32)
            tbuf[...] = jnp.dot(
                qs[...], oft[...], preferred_element_type=f32, precision=lax.Precision.HIGHEST
            )
            per = jnp.zeros((nq, tokens), f32)
            for i in range(hr):
                per = per + tbuf[i * nq:(i + 1) * nq, :] * ifs[i:i + 1, :]
            labels = lax.broadcasted_iota(jnp.int32, (EXAMPLES, tokens), 0).astype(f32)
            mask = jnp.where(labels == idrow[...], 1.0, 0.0)
            part = lax.dot_general(
                per, mask, NT, preferred_element_type=f32, precision=lax.Precision.HIGHEST
            )
            pb[...] = jnp.zeros_like(pb)
            pb[:, 0:EXAMPLES] = part

    def small_last(s):
        @pl.when((s == 4 + z) & has[0])
        def _():
            if_up().start()

        @pl.when((s == 4 + nz - 1 - z) & has[1])
        def _():
            if_dn().start()

    def step(s, carry):
        cc = s - lag
        slot = lax.rem(jnp.maximum(cc, 0), 2)
        on = cc >= 0

        for h in range(nz - 1, 2, -1):
            hop(h, s - h + 1)

        @pl.when(on)
        def _():
            finish(cc)
            load_w(cc, slot).wait()
            grads(cc, slot, 0)

        hop(2, s - 1)
        hop(1, s)

        @pl.when(s + AHEAD < pieces)
        def _():
            send_own(s + AHEAD)

        @pl.when(cc == pieces - 2)
        def _():
            core_acc(0).start()

        @pl.when(on)
        def _():
            grads(cc, slot, 1)

            @pl.when(cc + 2 < pieces - 1)
            def _():
                load_w(cc + 2, slot).start()

        small_first(s)

        @pl.when(on & (cc < early))
        def _():
            weights(cc, 0)

        cross(s - 1)

        @pl.when(on & (cc < early))
        def _():
            weights(cc, 1)

        small_last(s)
        return carry

    lax.fori_loop(0, steps, step, 0)

    core_acc(1).start()
    core_pb().start()
    finish(pieces - 1)
    core_gx().start()

    core_wx().wait()
    loads[6]().wait()
    core_ht().wait_send()
    core_of().wait_send()
    core_side().wait_send()
    if_x().wait_send()

    def drain(s, carry):
        for d in (0, 1):
            @pl.when(has[d])
            def _():
                own_z(d, s).wait_send()
                by_parity(s, lambda odd: fwd_a(d, s, odd).wait_send())
            for h in range(1, nz):
                @pl.when(there(d, h))
                def _():
                    if h < nz - 1:
                        @pl.when(has[d])
                        def _():
                            fwd_z(d, h, s).wait_send()
                    if h == 1:
                        by_parity(s, lambda odd: fwd_x(d, h, s, odd).wait_send())
                    else:
                        fwd_x(d, h, s, 0).wait_send()
        own_x(s).wait_send()
        return carry

    lax.fori_loop(0, pieces, drain, 0)
    for d in (0, 1):
        @pl.when(has[d])
        def _():
            t_own_z(d).wait_send()
            (if_up, if_dn)[d]().wait_send()
        for h in range(1, nz):
            @pl.when(there(d, h))
            def _():
                if h < nz - 1:
                    @pl.when(has[d])
                    def _():
                        t_fwd_z(d, h).wait_send()
                t_fwd_x(d, h).wait_send()
    t_own_x().wait_send()

    core_pb().wait()
    share = nq // 2
    sc[...] = pb[pl.ds(pl.multiple_of(c * share, 8), share), :] + pbx[...]
    for k in (0, 1):
        core_acc(k).wait()
    core_gx().wait()


def finish_kernel(G, ht, wgp, acc, rcv, wl, wx, gx, sc, wg, gh, scores, stage, ghb, sems, gsem):
    f32 = jnp.float32
    pieces, tokens, width = G.shape
    ff = ht.shape[0]
    half = tokens // 2
    early = wgp.shape[0]
    tile = ff // 2
    c = lax.axis_index("col")

    def out(s, src):
        return pltpu.make_async_copy(src, wg.at[:, pl.ds(s * width, width)], sems.at[s])

    for s in range(early):
        out(s, wgp.at[s]).start()
    for s in range(early, pieces):
        @pl.loop(0, 2)
        def _(k):
            r = pl.ds(pl.multiple_of(k * tile, 16), tile)
            stage[s - early, r, :] = jnp.dot(
                ht[r, :], G[s], preferred_element_type=f32
            ).astype(stage.dtype)
        out(s, stage.at[s - early]).start()
    mine = pl.ds(pl.multiple_of(c * half, 16), half)

    @pl.loop(0, 2)
    def _(k):
        r = pl.ds(pl.multiple_of(k * tile, 16), tile)
        t = acc[c, r, :] + rcv[r, :]
        t = t + lax.dot_general(wl[r, :], G[pieces - 1, mine, :], NT, preferred_element_type=f32)
        t = t + lax.dot_general(wx[r, :], gx[...], NT, preferred_element_type=f32)
        ghb[r, :] = t.astype(ghb.dtype)
        pltpu.make_async_copy(ghb.at[r], gh.at[r], gsem.at[k]).start()
    scores[...] = sc[:, 0:scores.shape[1]]
    for k in range(2):
        r = pl.ds(k * tile, tile)
        pltpu.make_async_copy(ghb.at[r], gh.at[r], gsem.at[k]).wait()
    for s in range(pieces):
        out(s, wgp.at[s] if s < early else stage.at[s - early]).wait()


def fused_body(grad_out, hidden_act, down_weight, proj_in, proj_out, queries, example_ids):
    bf16, f32, dma = jnp.bfloat16, jnp.float32, pltpu.SemaphoreType.DMA
    n = lax.axis_size("row")
    nz = n // 2
    rows_of, depth = grad_out.shape
    tokens = n * rows_of
    half, ff = hidden_act.shape
    width = depth // PIECES
    rank = proj_in.shape[1]
    hr = rank // 2
    nq = queries.shape[0]
    vm = pltpu.VMEM
    v_spec = pl.BlockSpec(memory_space=pltpu.VMEM)
    h_spec = pl.BlockSpec(memory_space=pltpu.HBM)

    args = (
        grad_out, hidden_act.T, down_weight, proj_in.T, proj_out.T, queries, example_ids.reshape(1, -1)
    )
    args = tuple(pltpu.with_memory_space_constraint(a, pltpu.HBM) for a in args)
    held = pl.pallas_call(
        functools.partial(gather_kernel, n),
        in_specs=[h_spec] * 7,
        out_specs=(v_spec,) * 9,
        out_shape=(
            vm((PIECES, tokens, width), bf16),
            vm((ff, tokens), bf16),
            vm((EARLY, ff, width), bf16),
            vm((2, ff, half), f32),
            vm((ff, half), f32),
            vm((ff, width), bf16),
            vm((ff, width), bf16),
            vm((half, width), bf16),
            vm((nq // 2, 128), f32),
        ),
        scratch_shapes=[
            vm((2, ff, width), bf16),
            vm((rows_of, depth), bf16),
            vm((hr, ff), bf16),
            vm((rank, depth), bf16),
            vm((nq, hr * rank), bf16),
            vm((1, rows_of), jnp.int32),
            vm((rank, rows_of), f32),
            vm((rank, rows_of), f32),
        ] + [vm((hr, tokens), f32)] * 7 + [
            vm((hr // 2 + 8, 2 * rows_of), f32),
            vm((n, hr // 2 + 8, 2 * rows_of), f32),
            vm((n, hr // 2 + 8, 2 * rows_of), f32),
            vm((rank, tokens), f32),
            vm((1, tokens), f32),
            vm((hr * nq, rank), f32),
            vm((hr * nq, tokens), f32),
            vm((nq, 128), f32),
            vm((nq // 2, 128), f32),
            dma((3, PIECES)),
            dma((2, nz - 2, PIECES)),
            dma((2, nz - 1, PIECES)),
            dma((2, PIECES)),
            dma((2, nz - 1, PIECES)),
            dma((2, nz - 1, PIECES)),
            dma((PIECES,)),
            dma((2, PIECES)),
            dma((3,)),
            dma((2, nz - 2)),
            dma((2, nz - 1)),
            dma((2, nz - 1)),
            dma((2, nz - 1)),
            dma((1,)),
            dma((PIECES,)),
            dma((2,)),
            dma((8,)),
            dma((7,)),
            dma((7,)),
            dma((5,)),
            dma((5,)),
        ],
        compiler_params=pltpu.CompilerParams(
            collective_id=0, has_side_effects=True, vmem_limit_bytes=12 << 20
        ),
    )(*args)

    wg, gh, scores = pl.pallas_call(
        finish_kernel,
        in_specs=[v_spec] * 9,
        out_specs=(h_spec, h_spec, v_spec),
        out_shape=(
            jax.ShapeDtypeStruct((ff, depth), bf16),
            jax.ShapeDtypeStruct((ff, half), bf16),
            jax.ShapeDtypeStruct((nq // 2, EXAMPLES), f32),
        ),
        scratch_shapes=[
            vm((PIECES - EARLY, ff, width), bf16),
            vm((ff, half), bf16),
            dma((PIECES,)),
            dma((2,)),
        ],
        compiler_params=pltpu.CompilerParams(vmem_limit_bytes=12 << 20),
    )(*held)
    return (gh.T, wg, scores)


def fits(mesh, shapes):
    n = mesh.shape["row"]
    if mesh.shape["col"] != 2 or n % 2 or not 6 <= n <= 16 or PIECES < n // 2 + 4:
        return False
    grad_out, hidden_act, _, proj_in, _, queries, _ = shapes
    parts = mesh.shape["grp"]
    rows_of = grad_out[0] // (parts * n)
    ff = hidden_act[1] // n
    rank = proj_in[1]
    return (
        2 * rows_of == 128
        and grad_out[1] % (2 * PIECES * 256) == 0
        and ff % 64 == 0
        and rank % 32 == 0
        and queries[0] % (16 * n) == 0
        and queries[1] == rank * rank
        and ff * (rows_of * n + grad_out[1]) < 24 << 20
    )


def solution(mesh):
    def run(*args):
        body = fused_body if fits(mesh, [a.shape for a in args]) else plain_body
        return jax.shard_map(
            body,
            mesh=mesh,
            in_specs=(
                P(("grp", "row"), "col"),
                P(("grp", "col"), "row"),
                P("row", "col"),
                P("row", None),
                P("col", None),
                P("row", "col"),
                P(("grp", "row")),
            ),
            out_specs=(P(("grp", "col"), "row"), P(("grp", "row"), "col"), P(("row", "col"), "grp")),
            check_vma=False,
        )(*args)

    return run
```

```python
import functools

import jax
import jax.numpy as jnp
from jax import lax
from jax.experimental import pallas as pl
from jax.experimental.pallas import tpu as pltpu
from jax.sharding import PartitionSpec as P

EXAMPLES = 8
CHUNKS = 4
PIECES = 8
AHEAD = 2
EARLY = 5

MESH = pl.DeviceIdType.MESH
NT = (((1,), (1,)), ((), ()))


def swap(x, axis, bit):
    n = lax.axis_size(axis)
    return lax.ppermute(x, axis, [(i, i ^ bit) for i in range(n)])


def pair_order(own, other, index, axis):
    first = jnp.where(index == 0, own, other)
    second = jnp.where(index == 0, other, own)
    return jnp.concatenate([first, second], axis=axis)


def gather_rows(block):
    n = lax.axis_size("row")
    if n % 2 or n > 16:
        return lax.all_gather(block, "row", axis=0, tiled=True)
    outer = n // 2
    me = lax.axis_index("row")
    z, x = me // 2, me % 2
    held = [block]
    for k in range(1, outer):
        perm = [(i, ((i // 2 + k) % outer) * 2 + i % 2) for i in range(n)]
        held.append(lax.ppermute(block, "row", perm))
    mine = jnp.stack(held[::-1])
    theirs = swap(mine, "row", 1)
    both = pair_order(mine, theirs, x, 1)
    twice = jnp.concatenate([both, both], axis=0)
    rows = lax.dynamic_slice_in_dim(twice, outer - 1 - z, outer, 0)
    return rows.reshape((n * block.shape[0],) + block.shape[1:])


def sum_rows(x):
    n = lax.axis_size("row")
    if n & (n - 1):
        return lax.psum(x, "row")
    bit = 1
    while bit < n:
        x = x + swap(x, "row", bit)
        bit *= 2
    return x


def product_kernel(a_ref, b_ref, *refs):
    out_ref = refs[-1]
    out_ref[...] = jnp.dot(
        a_ref[...], b_ref[...], preferred_element_type=jnp.float32
    ).astype(out_ref.dtype)


def product_into(a, b, total, at, chunks):
    rows, depth = a.shape
    width = b.shape[1]
    tile = rows
    for parts in (8, 4, 2):
        if rows % (parts * 16) == 0:
            tile = rows // parts
            break
    in_specs = [
        pl.BlockSpec((tile, depth), lambda i: (i, 0)),
        pl.BlockSpec((depth, width), lambda i: (0, 0)),
    ]
    args = (a, b)
    aliases = {}
    if total is not None:
        in_specs.append(pl.BlockSpec(memory_space=pl.ANY))
        args = (a, b, total)
        aliases = {2: 0}
    return pl.pallas_call(
        product_kernel,
        grid=(rows // tile,),
        in_specs=in_specs,
        out_specs=pl.BlockSpec((tile, width), lambda i: (i, at)),
        out_shape=jax.ShapeDtypeStruct((rows, chunks * width), jnp.bfloat16),
        input_output_aliases=aliases,
        compiler_params=pltpu.CompilerParams(vmem_limit_bytes=24 << 20),
        cost_estimate=pl.CostEstimate(
            flops=2 * rows * depth * width,
            bytes_accessed=2 * (rows * depth + depth * width + rows * width),
            transcendentals=0,
        ),
    )(*args)


def plain_body(grad_out, hidden_act, down_weight, proj_in, proj_out, queries, example_ids):
    f32 = jnp.float32
    col = lax.axis_index("col")
    half_rank = proj_in.shape[1] // lax.axis_size("col")

    width = grad_out.shape[1] // CHUNKS
    parts = [
        gather_rows(lax.slice_in_dim(grad_out, c * width, (c + 1) * width, axis=1))
        for c in range(CHUNKS)
    ]

    other_hidden = swap(hidden_act, "col", 1)
    full_hidden = pair_order(hidden_act, other_hidden, col, 0)
    hidden_t = full_hidden.T

    own_proj = lax.dynamic_slice_in_dim(proj_in, col * half_rank, half_rank, 1)
    in_factor = sum_rows(
        lax.dot_general(own_proj, full_hidden, (((0,), (1,)), ((), ())), preferred_element_type=f32)
    )

    out_own = lax.dot_general(
        proj_out, grad_out, (((0,), (1,)), ((), ())), preferred_element_type=f32
    ).T
    out_own = out_own + swap(out_own, "col", 1)
    packed = gather_rows(jnp.concatenate([out_own, example_ids[:, None].astype(f32)], axis=1))
    out_factor = packed[:, :-1]
    ids = packed[:, -1].astype(jnp.int32)
    labels = jnp.arange(EXAMPLES, dtype=jnp.int32)
    onehot = ids[None, :] == labels[:, None]
    masked = jnp.where(onehot[:, None, :], in_factor[None], 0.0)
    example_grads = jnp.dot(
        masked.reshape(EXAMPLES * half_rank, -1), out_factor, precision=lax.Precision.HIGHEST
    ).reshape(EXAMPLES, -1)
    values = lax.dot_general(
        queries.astype(f32), example_grads, (((1,), (1,)), ((), ())), precision=lax.Precision.HIGHEST
    )
    share = values.shape[0] // 2
    keep = lax.dynamic_slice_in_dim(values, col * share, share, 0)
    send = lax.dynamic_slice_in_dim(values, (1 - col) * share, share, 0)
    scores = keep + swap(send, "col", 1)

    total = None
    weight_grad = None
    for c in range(CHUNKS):
        weights = lax.slice_in_dim(down_weight, c * width, (c + 1) * width, axis=1)
        term = lax.dot_general(
            parts[c], weights, (((1,), (1,)), ((), ())), preferred_element_type=f32
        )
        total = term if total is None else total + term
        weight_grad = product_into(hidden_t, parts[c], weight_grad, c, CHUNKS)
    tokens = total.shape[0] // 2
    keep = lax.dynamic_slice_in_dim(total, col * tokens, tokens, 0)
    send = lax.dynamic_slice_in_dim(total, (1 - col) * tokens, tokens, 0)
    grad_hidden = (keep + swap(send, "col", 1)).astype(jnp.bfloat16)
    return (grad_hidden, weight_grad, scores)


def gather_kernel(
    n,
    g, hto, w, pin, pout, q, ids,
    G, ht, wgp, acc, rcv, wl, wx, gx, sc,
    wbuf, gown, pin_v, pout_v, q_v, ids_v, ofo, ofx, ifp, ift, ifx, ifs,
    pu, pd, pur, pdr, side_src, side, sidex, oft, idrow, qs, tbuf, pb, pbx,
    s_own, s_fz, s_fx, s_a, r_z, r_x, r_xo, r_a,
    t_own, t_fz, t_fx, u_z, u_x, u_xo,
    l_own, l_w, l_misc, c_send, c_recv, k_send, k_recv,
):
    f32 = jnp.float32
    pieces, tokens, width = G.shape
    rows_of = tokens // n
    ff = ht.shape[0]
    half = tokens // 2
    quarter = width // 4
    nz = n // 2
    lag = nz - 1
    steps = pieces + lag - 1
    tile = ff // 2
    hr = pin_v.shape[0]
    rank = pout_v.shape[0]
    early = wgp.shape[0]
    nq = q_v.shape[0]

    me = lax.axis_index("row")
    c = lax.axis_index("col")
    z, x = me // 2, me % 2
    has = (z < nz - 1, z > 0)
    nxt = ({"row": me + 2}, {"row": me - 2})
    xp = {"row": me + 1 - 2 * x}
    cp = {"col": 1 - c}

    def rc(src, dst, send, recv, dev):
        return pltpu.make_async_remote_copy(
            src_ref=src, dst_ref=dst, send_sem=send, recv_sem=recv, device_id=dev, device_id_type=MESH
        )

    def lc(src, dst, sem):
        return pltpu.make_async_copy(src, dst, sem)

    def rows(b):
        return pl.ds(pl.multiple_of(b * rows_of, 16), rows_of)

    def cols(s):
        return pl.ds(pl.multiple_of(s * width, 128), width)

    def at_z(d, h):
        return z - h if d == 0 else z + h

    def there(d, h):
        return z >= h if d == 0 else z + h < nz

    def own_z(d, s):
        return rc(g.at[:, cols(s)], G.at[s, rows(me)], s_own.at[d, s], r_z.at[d, 0, s], nxt[d])

    def own_x(s):
        return rc(g.at[:, cols(s)], G.at[s, rows(me)], s_own.at[2, s], r_xo.at[s], xp)

    def fwd_z(d, h, s):
        part = G.at[s, rows(at_z(d, h) * 2 + x)]
        return rc(part, part, s_fz.at[d, h - 1, s], r_z.at[d, h, s], nxt[d])

    def fwd_x(d, h, s, odd, other=False):
        xx = 1 - x if other else x
        r = rows(at_z(d, h) * 2 + xx)
        cut = quarter * (1 + odd)
        part = G.at[s, r, pl.ds(cut, width - cut)] if h == 1 else G.at[s, r]
        return rc(part, part, s_fx.at[d, h - 1, s], r_x.at[d, h - 1, s], xp)

    def fwd_a(d, s, odd):
        part = G.at[s, rows(z * 2 + 1 - x), pl.ds(0, quarter * (1 + odd))]
        return rc(part, part, s_a.at[d, s], r_a.at[d, s], nxt[d])

    def by_parity(s, f):
        for odd in (0, 1):
            @pl.when(lax.rem(s, 2) == odd)
            def _():
                f(odd)

    def got_z(d, h, s):
        part = G.at[s, rows(at_z(d, h) * 2 + x)]
        return rc(part, part, s_own.at[d, s], r_z.at[d, h - 1, s], nxt[d])

    def got_xo(s):
        part = G.at[s, rows(z * 2 + 1 - x)]
        return rc(part, part, s_own.at[2, s], r_xo.at[s], xp)

    def got_a(d, s, odd):
        part = G.at[s, rows(at_z(d, 1) * 2 + 1 - x), pl.ds(0, quarter * (1 + odd))]
        return rc(part, part, s_a.at[d, s], r_a.at[d, s], nxt[d])

    def t_own_z(d):
        return rc(side_src, side.at[me], t_own.at[d], u_z.at[d, 0], nxt[d])

    def t_own_x():
        return rc(side_src, side.at[me], t_own.at[2], u_xo.at[0], xp)

    def t_fwd_z(d, h):
        part = side.at[at_z(d, h) * 2 + x]
        return rc(part, part, t_fz.at[d, h - 1], u_z.at[d, h], nxt[d])

    def t_fwd_x(d, h, other=False):
        part = side.at[at_z(d, h) * 2 + (1 - x if other else x)]
        return rc(part, part, t_fx.at[d, h - 1], u_x.at[d, h - 1], xp)

    def t_got_z(d, h):
        part = side.at[at_z(d, h) * 2 + x]
        return rc(part, part, t_own.at[d], u_z.at[d, h - 1], nxt[d])

    def t_got_xo():
        part = side.at[z * 2 + 1 - x]
        return rc(part, part, t_own.at[2], u_xo.at[0], xp)

    def tok_half(ref, k):
        return ref.at[:, pl.ds(pl.multiple_of(k * half, 128), half)]

    def core_ht():
        return rc(hto, tok_half(ht, c), c_send.at[0], c_recv.at[0], cp)

    def core_wx():
        return rc(w.at[:, pl.ds((pieces - 1) * width, width)], wx, c_send.at[1], c_recv.at[1], cp)

    def core_of():
        return rc(ofo, ofx, c_send.at[2], c_recv.at[2], cp)

    def core_side():
        return rc(side, sidex, c_send.at[3], c_recv.at[3], cp)

    def core_acc(k):
        r = pl.ds(k * tile, tile)
        return rc(acc.at[1 - c, r], rcv.at[r], k_send.at[3 + k], k_recv.at[3 + k], cp)

    def core_gx():
        src = G.at[pieces - 1, pl.ds(pl.multiple_of((1 - c) * half, 16), half)]
        return rc(src, gx, c_send.at[5], c_recv.at[5], cp)

    def core_pb():
        share = nq // 2
        src = pb.at[pl.ds(pl.multiple_of((1 - c) * share, 8), share)]
        return rc(src, pbx, c_send.at[6], c_recv.at[6], cp)

    def x_half(ref, k):
        return ref.at[:, pl.ds(pl.multiple_of(k * half, 128), half)]

    def if_x():
        return rc(x_half(ifp, 1 - x), ifx, k_send.at[0], k_recv.at[0], xp)

    def if_back(other=False):
        part = x_half(ift, 1 - x if other else x)
        return rc(part, part, k_send.at[5], k_recv.at[5], xp)

    def if_up():
        return rc(pu, pur, k_send.at[1], k_recv.at[1], nxt[0])

    def if_dn():
        return rc(pd, pdr, k_send.at[2], k_recv.at[2], nxt[1])

    def load_own(s):
        return lc(g.at[:, cols(s)], G.at[s, rows(me)], l_own.at[s])

    def load_w(s, slot):
        return lc(w.at[:, cols(s)], wbuf.at[slot], l_w.at[slot])

    loads = (
        lambda: lc(g, gown, l_misc.at[0]),
        lambda: lc(pout, pout_v, l_misc.at[1]),
        lambda: lc(hto, tok_half(ht, c), l_misc.at[2]),
        lambda: lc(pin.at[pl.ds(pl.multiple_of(c * hr, 16), hr)], pin_v, l_misc.at[3]),
        lambda: lc(q, q_v, l_misc.at[4]),
        lambda: lc(ids, ids_v, l_misc.at[5]),
        lambda: lc(w.at[:, pl.ds((pieces - 1) * width, width)], wl, l_misc.at[6]),
    )

    barrier = pltpu.get_barrier_semaphore()
    for d in (0, 1):
        @pl.when(has[d])
        def _():
            pl.semaphore_signal(barrier, inc=1, device_id=nxt[d], device_id_type=MESH)
    pl.semaphore_signal(barrier, inc=1, device_id=xp, device_id_type=MESH)
    pl.semaphore_signal(barrier, inc=1, device_id=cp, device_id_type=MESH)
    for k in (0, 1, 2, 3, 4, 5):
        loads[k]().start()
    for s in range(2):
        load_w(s, s).start()
    pl.semaphore_wait(barrier, 2 + jnp.where(has[0], 1, 0) + jnp.where(has[1], 1, 0))

    def send_own(s):
        for d in (0, 1):
            @pl.when(has[d])
            def _():
                own_z(d, s).start()
        own_x(s).start()
        load_own(s).start()

    for s in range(AHEAD):
        send_own(s)
    core_ht().start()
    core_wx().start()
    loads[6]().start()

    def hop(h, s):
        @pl.when((s >= 0) & (s < pieces))
        def _():
            for d in (0, 1):
                @pl.when(there(d, h))
                def _():
                    got_z(d, h, s).wait_recv()
                    if h < nz - 1:
                        @pl.when(has[d])
                        def _():
                            fwd_z(d, h, s).start()
                    if h == 1:
                        by_parity(s, lambda odd: fwd_x(d, h, s, odd).start())
                    else:
                        fwd_x(d, h, s, 0).start()

    def cross(s):
        @pl.when((s >= 0) & (s < pieces))
        def _():
            got_xo(s).wait_recv()
            for d in (0, 1):
                @pl.when(has[d])
                def _():
                    by_parity(s, lambda odd: fwd_a(d, s, odd).start())

    def finish(s):
        load_own(s).wait()
        for d in (0, 1):
            for h in range(1, nz):
                @pl.when(there(d, h))
                def _():
                    if h == 1:
                        def both(odd):
                            fwd_x(d, h, s, odd, True).wait_recv()
                            got_a(d, s, odd).wait_recv()

                        by_parity(s, both)
                    else:
                        fwd_x(d, h, s, 0, True).wait_recv()

    def side_hop(h, s):
        @pl.when(s == 2 + h)
        def _():
            for d in (0, 1):
                @pl.when(there(d, h))
                def _():
                    t_got_z(d, h).wait_recv()
                    if h < nz - 1:
                        @pl.when(has[d])
                        def _():
                            t_fwd_z(d, h).start()
                    t_fwd_x(d, h).start()

    def grads(s, slot, k):
        r = pl.ds(pl.multiple_of(k * tile, 16), tile)
        t = lax.dot_general(wbuf[slot, r, :], G[s], NT, preferred_element_type=f32)
        acc[0, r, :] += t[:, :half]
        acc[1, r, :] += t[:, half:]

    def weights(s, k):
        r = pl.ds(pl.multiple_of(k * tile, 16), tile)
        wgp[s, r, :] = jnp.dot(ht[r, :], G[s], preferred_element_type=f32).astype(wgp.dtype)

    def thirds(v):
        a = v.astype(jnp.bfloat16)
        rest = v - a.astype(f32)
        b = rest.astype(jnp.bfloat16)
        return a, b, (rest - b.astype(f32)).astype(jnp.bfloat16)

    def small_first(s):
        hh = hr // 2

        @pl.when(s == 0)
        def _():
            loads[0]().wait()
            loads[1]().wait()
            ofo[...] = lax.dot_general(pout_v[...], gown[...], NT, preferred_element_type=f32)
            pur[...] = jnp.zeros_like(pur)
            pdr[...] = jnp.zeros_like(pdr)
            side_src[...] = jnp.zeros_like(side_src)
            acc[...] = jnp.zeros_like(acc)

        @pl.when(s == 1)
        def _():
            core_of().wait_recv()
            loads[5]().wait()
            mine = pl.ds(pl.multiple_of(c * hr, 8), hr)
            both = ofo[mine, :] + ofx[mine, :]
            side_src[0:hh, 0:rows_of] = both[:hh]
            side_src[0:hh, rows_of:2 * rows_of] = both[hh:]
            side_src[hh:hh + 1, 0:rows_of] = ids_v[...].astype(f32)
            loads[2]().wait()
            loads[3]().wait()
            core_ht().wait_recv()
            ifp[...] = jnp.dot(pin_v[...], ht[...], preferred_element_type=f32)

        @pl.when(s == 2)
        def _():
            loads[4]().wait()
            for i in range(hr):
                for k in range(3):
                    qs[i * nq:(i + 1) * nq, k * rank:(k + 1) * rank] = (
                        q_v[:, i * rank:(i + 1) * rank]
                    )
            if_x().wait_recv()
            mine = pl.ds(pl.multiple_of(x * half, 128), half)
            ifs[...] = ifp[:, mine] + ifx[...]

        @pl.when((s == 3 + z) & has[0])
        def _():
            @pl.when(z > 0)
            def _():
                if_up().wait_recv()
            pu[...] = ifs[...] + pur[...]

        @pl.when((s == 2 + nz - z) & has[1])
        def _():
            @pl.when(z < nz - 1)
            def _():
                if_dn().wait_recv()
            pd[...] = ifs[...] + pdr[...]

        for h in range(1, nz):
            side_hop(h, s)

        @pl.when(s == 3 + nz)
        def _():
            lc(side_src, side.at[me], l_misc.at[7]).wait()
            t_got_xo().wait_recv()
            for d in (0, 1):
                for h in range(1, nz):
                    @pl.when(there(d, h))
                    def _():
                        t_fwd_x(d, h, True).wait_recv()
            core_side().start()

            @pl.when(z == nz - 1)
            def _():
                if_up().wait_recv()

            @pl.when(z == 0)
            def _():
                if_dn().wait_recv()
            mine = pl.ds(pl.multiple_of(x * half, 128), half)
            ift[:, mine] = ifs[...] + pur[...] + pdr[...]

        @pl.when(s == 4 + nz)
        def _():
            core_side().wait_recv()
            if_back(True).wait_recv()
            mine = pl.multiple_of(c * hr, 8)
            others = pl.multiple_of((1 - c) * hr, 8)
            for b in range(n):
                t = slice(b * rows_of, (b + 1) * rows_of)
                for k in (0, 1):
                    lanes = slice(k * rows_of, (k + 1) * rows_of)
                    oft[pl.ds(mine + k * hh, hh), t] = side[b, 0:hh, lanes]
                    oft[pl.ds(others + k * hh, hh), t] = sidex[b, 0:hh, lanes]
                idrow[0:1, t] = side[b, hh:hh + 1, 0:rows_of]
            tbuf[...] = jnp.dot(
                qs[...], jnp.concatenate(thirds(oft[...]), axis=0), preferred_element_type=f32
            )
            per = jnp.zeros((nq, tokens), f32)
            for i in range(hr):
                per = per + tbuf[i * nq:(i + 1) * nq, :] * ift[i:i + 1, :]
            labels = lax.broadcasted_iota(jnp.int32, (EXAMPLES, tokens), 0).astype(f32)
            mask = jnp.where(labels == idrow[...], 1.0, 0.0).astype(jnp.bfloat16)
            part = lax.dot_general(
                jnp.concatenate(thirds(per), axis=0), mask, NT, preferred_element_type=f32
            )
            pb[...] = jnp.zeros_like(pb)
            pb[:, 0:EXAMPLES] = part[:nq] + part[nq:2 * nq] + part[2 * nq:]

    def small_last(s):
        @pl.when(s == 0)
        def _():
            core_of().start()

        @pl.when(s == 1)
        def _():
            for d in (0, 1):
                @pl.when(has[d])
                def _():
                    t_own_z(d).start()
            t_own_x().start()
            lc(side_src, side.at[me], l_misc.at[7]).start()
            if_x().start()

        @pl.when((s == 3 + z) & has[0])
        def _():
            if_up().start()

        @pl.when((s == 2 + nz - z) & has[1])
        def _():
            if_dn().start()

        @pl.when(s == 3 + nz)
        def _():
            if_back().start()

    def drain(s):
        for d in (0, 1):
            @pl.when(has[d])
            def _():
                own_z(d, s).wait_send()
                by_parity(s, lambda odd: fwd_a(d, s, odd).wait_send())
            for h in range(1, nz):
                @pl.when(there(d, h))
                def _():
                    if h < nz - 1:
                        @pl.when(has[d])
                        def _():
                            fwd_z(d, h, s).wait_send()
                    if h == 1:
                        by_parity(s, lambda odd: fwd_x(d, h, s, odd).wait_send())
                    else:
                        fwd_x(d, h, s, 0).wait_send()
        own_x(s).wait_send()

    def step(s, carry):
        cc = s - lag
        slot = lax.rem(jnp.maximum(cc, 0), 2)
        on = cc >= 0

        for h in range(nz - 1, 2, -1):
            hop(h, s - h + 1)

        @pl.when(on)
        def _():
            finish(cc)
            load_w(cc, slot).wait()
            grads(cc, slot, 0)

        hop(2, s - 1)
        hop(1, s)

        @pl.when(s + AHEAD < pieces)
        def _():
            send_own(s + AHEAD)

        @pl.when(cc == pieces - 2)
        def _():
            core_acc(0).start()

        @pl.when(on)
        def _():
            grads(cc, slot, 1)

            @pl.when(cc + 2 < pieces - 1)
            def _():
                load_w(cc + 2, slot).start()

        small_first(s)

        @pl.when(on & (cc < early))
        def _():
            weights(cc, 0)

        cross(s - 1)

        @pl.when(on & (cc < early))
        def _():
            weights(cc, 1)

        small_last(s)

        @pl.when(cc >= 2)
        def _():
            drain(cc - 2)
        return carry

    lax.fori_loop(0, steps, step, 0)

    core_acc(1).start()
    core_pb().start()
    finish(pieces - 1)
    core_gx().start()

    core_wx().wait()
    loads[6]().wait()
    core_ht().wait_send()
    core_of().wait_send()
    core_side().wait_send()
    if_x().wait_send()
    if_back().wait_send()

    pl.loop(steps - lag - 2, pieces)(drain)
    for d in (0, 1):
        @pl.when(has[d])
        def _():
            t_own_z(d).wait_send()
            (if_up, if_dn)[d]().wait_send()
        for h in range(1, nz):
            @pl.when(there(d, h))
            def _():
                if h < nz - 1:
                    @pl.when(has[d])
                    def _():
                        t_fwd_z(d, h).wait_send()
                t_fwd_x(d, h).wait_send()
    t_own_x().wait_send()

    core_pb().wait()
    share = nq // 2
    sc[...] = pb[pl.ds(pl.multiple_of(c * share, 8), share), :] + pbx[...]
    for k in (0, 1):
        core_acc(k).wait()
    core_gx().wait()


def finish_kernel(G, ht, wgp, acc, rcv, wl, wx, gx, sc, wg, gh, scores, stage, ghb, sems, gsem):
    f32 = jnp.float32
    pieces, tokens, width = G.shape
    ff = ht.shape[0]
    half = tokens // 2
    early = wgp.shape[0]
    tile = ff // 2
    c = lax.axis_index("col")

    def out(s, src):
        return pltpu.make_async_copy(src, wg.at[:, pl.ds(s * width, width)], sems.at[s])

    for s in range(early):
        out(s, wgp.at[s]).start()
    for s in range(early, pieces):
        @pl.loop(0, 2)
        def _(k):
            r = pl.ds(pl.multiple_of(k * tile, 16), tile)
            stage[s - early, r, :] = jnp.dot(
                ht[r, :], G[s], preferred_element_type=f32
            ).astype(stage.dtype)
        out(s, stage.at[s - early]).start()
    mine = pl.ds(pl.multiple_of(c * half, 16), half)

    @pl.loop(0, 2)
    def _(k):
        r = pl.ds(pl.multiple_of(k * tile, 16), tile)
        t = acc[c, r, :] + rcv[r, :]
        t = t + lax.dot_general(wl[r, :], G[pieces - 1, mine, :], NT, preferred_element_type=f32)
        t = t + lax.dot_general(wx[r, :], gx[...], NT, preferred_element_type=f32)
        ghb[r, :] = t.astype(ghb.dtype)
        pltpu.make_async_copy(ghb.at[r], gh.at[r], gsem.at[k]).start()
    scores[...] = sc[:, 0:scores.shape[1]]
    for k in range(2):
        r = pl.ds(k * tile, tile)
        pltpu.make_async_copy(ghb.at[r], gh.at[r], gsem.at[k]).wait()
    for s in range(pieces):
        out(s, wgp.at[s] if s < early else stage.at[s - early]).wait()


def fused_body(grad_out, hidden_act, down_weight, proj_in, proj_out, queries, example_ids):
    bf16, f32, dma = jnp.bfloat16, jnp.float32, pltpu.SemaphoreType.DMA
    n = lax.axis_size("row")
    nz = n // 2
    rows_of, depth = grad_out.shape
    tokens = n * rows_of
    half, ff = hidden_act.shape
    width = depth // PIECES
    rank = proj_in.shape[1]
    hr = rank // 2
    nq = queries.shape[0]
    vm = pltpu.VMEM
    v_spec = pl.BlockSpec(memory_space=pltpu.VMEM)
    h_spec = pl.BlockSpec(memory_space=pltpu.HBM)

    args = (
        grad_out, hidden_act.T, down_weight, proj_in.T, proj_out.T, queries, example_ids.reshape(1, -1)
    )
    args = tuple(pltpu.with_memory_space_constraint(a, pltpu.HBM) for a in args)
    held = pl.pallas_call(
        functools.partial(gather_kernel, n),
        in_specs=[h_spec] * 7,
        out_specs=(v_spec,) * 9,
        out_shape=(
            vm((PIECES, tokens, width), bf16),
            vm((ff, tokens), bf16),
            vm((EARLY, ff, width), bf16),
            vm((2, ff, half), f32),
            vm((ff, half), f32),
            vm((ff, width), bf16),
            vm((ff, width), bf16),
            vm((half, width), bf16),
            vm((nq // 2, 128), f32),
        ),
        scratch_shapes=[
            vm((2, ff, width), bf16),
            vm((rows_of, depth), bf16),
            vm((hr, ff), bf16),
            vm((rank, depth), bf16),
            vm((nq, hr * rank), bf16),
            vm((1, rows_of), jnp.int32),
            vm((rank, rows_of), f32),
            vm((rank, rows_of), f32),
        ] + [vm((hr, tokens), f32)] * 2 + [vm((hr, half), f32)] * 6 + [
            vm((hr // 2 + 1, 2 * rows_of), f32),
            vm((n, hr // 2 + 1, 2 * rows_of), f32),
            vm((n, hr // 2 + 1, 2 * rows_of), f32),
            vm((rank, tokens), f32),
            vm((1, tokens), f32),
            vm((hr * nq, 3 * rank), bf16),
            vm((hr * nq, tokens), f32),
            vm((nq, 128), f32),
            vm((nq // 2, 128), f32),
            dma((3, PIECES)),
            dma((2, nz - 2, PIECES)),
            dma((2, nz - 1, PIECES)),
            dma((2, PIECES)),
            dma((2, nz - 1, PIECES)),
            dma((2, nz - 1, PIECES)),
            dma((PIECES,)),
            dma((2, PIECES)),
            dma((3,)),
            dma((2, nz - 2)),
            dma((2, nz - 1)),
            dma((2, nz - 1)),
            dma((2, nz - 1)),
            dma((1,)),
            dma((PIECES,)),
            dma((2,)),
            dma((8,)),
            dma((7,)),
            dma((7,)),
            dma((6,)),
            dma((6,)),
        ],
        compiler_params=pltpu.CompilerParams(
            collective_id=0, has_side_effects=True, vmem_limit_bytes=12 << 20
        ),
    )(*args)

    wg, gh, scores = pl.pallas_call(
        finish_kernel,
        in_specs=[v_spec] * 9,
        out_specs=(h_spec, h_spec, v_spec),
        out_shape=(
            jax.ShapeDtypeStruct((ff, depth), bf16),
            jax.ShapeDtypeStruct((ff, half), bf16),
            jax.ShapeDtypeStruct((nq // 2, EXAMPLES), f32),
        ),
        scratch_shapes=[
            vm((PIECES - EARLY, ff, width), bf16),
            vm((ff, half), bf16),
            dma((PIECES,)),
            dma((2,)),
        ],
        compiler_params=pltpu.CompilerParams(vmem_limit_bytes=12 << 20),
    )(*held)
    return (gh.T, wg, scores)


def fits(mesh, shapes):
    n = mesh.shape["row"]
    if mesh.shape["col"] != 2 or n % 2 or not 6 <= n <= 16 or PIECES < n // 2 + 4:
        return False
    grad_out, hidden_act, _, proj_in, _, queries, _ = shapes
    parts = mesh.shape["grp"]
    rows_of = grad_out[0] // (parts * n)
    ff = hidden_act[1] // n
    rank = proj_in[1]
    return (
        2 * rows_of == 128
        and grad_out[1] % (2 * PIECES * 256) == 0
        and ff % 64 == 0
        and rank % 32 == 0
        and queries[0] % (16 * n) == 0
        and queries[1] == rank * rank
        and ff * (rows_of * n + grad_out[1]) < 24 << 20
    )


def solution(mesh):
    def run(*args):
        body = fused_body if fits(mesh, [a.shape for a in args]) else plain_body
        return jax.shard_map(
            body,
            mesh=mesh,
            in_specs=(
                P(("grp", "row"), "col"),
                P(("grp", "col"), "row"),
                P("row", "col"),
                P("row", None),
                P("col", None),
                P("row", "col"),
                P(("grp", "row")),
            ),
            out_specs=(P(("grp", "col"), "row"), P(("grp", "row"), "col"), P(("row", "col"), "grp")),
            check_vma=False,
        )(*args)

    return run
```

```python
import functools

import jax
import jax.numpy as jnp
from jax import lax
from jax.experimental import pallas as pl
from jax.experimental.pallas import tpu as pltpu
from jax.sharding import PartitionSpec as P

EXAMPLES = 8
CHUNKS = 4
PIECES = 8
AHEAD = 3
EARLY = 6
LATE = 2

MESH = pl.DeviceIdType.MESH
NT = (((1,), (1,)), ((), ()))


def swap(x, axis, bit):
    n = lax.axis_size(axis)
    return lax.ppermute(x, axis, [(i, i ^ bit) for i in range(n)])


def pair_order(own, other, index, axis):
    first = jnp.where(index == 0, own, other)
    second = jnp.where(index == 0, other, own)
    return jnp.concatenate([first, second], axis=axis)


def gather_rows(block):
    n = lax.axis_size("row")
    if n % 2 or n > 16:
        return lax.all_gather(block, "row", axis=0, tiled=True)
    outer = n // 2
    me = lax.axis_index("row")
    z, x = me // 2, me % 2
    held = [block]
    for k in range(1, outer):
        perm = [(i, ((i // 2 + k) % outer) * 2 + i % 2) for i in range(n)]
        held.append(lax.ppermute(block, "row", perm))
    mine = jnp.stack(held[::-1])
    theirs = swap(mine, "row", 1)
    both = pair_order(mine, theirs, x, 1)
    twice = jnp.concatenate([both, both], axis=0)
    rows = lax.dynamic_slice_in_dim(twice, outer - 1 - z, outer, 0)
    return rows.reshape((n * block.shape[0],) + block.shape[1:])


def sum_rows(x):
    n = lax.axis_size("row")
    if n & (n - 1):
        return lax.psum(x, "row")
    bit = 1
    while bit < n:
        x = x + swap(x, "row", bit)
        bit *= 2
    return x


def product_kernel(a_ref, b_ref, *refs):
    out_ref = refs[-1]
    out_ref[...] = jnp.dot(
        a_ref[...], b_ref[...], preferred_element_type=jnp.float32
    ).astype(out_ref.dtype)


def product_into(a, b, total, at, chunks):
    rows, depth = a.shape
    width = b.shape[1]
    tile = rows
    for parts in (8, 4, 2):
        if rows % (parts * 16) == 0:
            tile = rows // parts
            break
    in_specs = [
        pl.BlockSpec((tile, depth), lambda i: (i, 0)),
        pl.BlockSpec((depth, width), lambda i: (0, 0)),
    ]
    args = (a, b)
    aliases = {}
    if total is not None:
        in_specs.append(pl.BlockSpec(memory_space=pl.ANY))
        args = (a, b, total)
        aliases = {2: 0}
    return pl.pallas_call(
        product_kernel,
        grid=(rows // tile,),
        in_specs=in_specs,
        out_specs=pl.BlockSpec((tile, width), lambda i: (i, at)),
        out_shape=jax.ShapeDtypeStruct((rows, chunks * width), jnp.bfloat16),
        input_output_aliases=aliases,
        compiler_params=pltpu.CompilerParams(vmem_limit_bytes=24 << 20),
        cost_estimate=pl.CostEstimate(
            flops=2 * rows * depth * width,
            bytes_accessed=2 * (rows * depth + depth * width + rows * width),
            transcendentals=0,
        ),
    )(*args)


def plain_body(grad_out, hidden_act, down_weight, proj_in, proj_out, queries, example_ids):
    f32 = jnp.float32
    col = lax.axis_index("col")
    half_rank = proj_in.shape[1] // lax.axis_size("col")

    width = grad_out.shape[1] // CHUNKS
    parts = [
        gather_rows(lax.slice_in_dim(grad_out, c * width, (c + 1) * width, axis=1))
        for c in range(CHUNKS)
    ]

    other_hidden = swap(hidden_act, "col", 1)
    full_hidden = pair_order(hidden_act, other_hidden, col, 0)
    hidden_t = full_hidden.T

    own_proj = lax.dynamic_slice_in_dim(proj_in, col * half_rank, half_rank, 1)
    in_factor = sum_rows(
        lax.dot_general(own_proj, full_hidden, (((0,), (1,)), ((), ())), preferred_element_type=f32)
    )

    out_own = lax.dot_general(
        proj_out, grad_out, (((0,), (1,)), ((), ())), preferred_element_type=f32
    ).T
    out_own = out_own + swap(out_own, "col", 1)
    packed = gather_rows(jnp.concatenate([out_own, example_ids[:, None].astype(f32)], axis=1))
    out_factor = packed[:, :-1]
    ids = packed[:, -1].astype(jnp.int32)
    labels = jnp.arange(EXAMPLES, dtype=jnp.int32)
    onehot = ids[None, :] == labels[:, None]
    masked = jnp.where(onehot[:, None, :], in_factor[None], 0.0)
    example_grads = jnp.dot(
        masked.reshape(EXAMPLES * half_rank, -1), out_factor, precision=lax.Precision.HIGHEST
    ).reshape(EXAMPLES, -1)
    values = lax.dot_general(
        queries.astype(f32), example_grads, (((1,), (1,)), ((), ())), precision=lax.Precision.HIGHEST
    )
    share = values.shape[0] // 2
    keep = lax.dynamic_slice_in_dim(values, col * share, share, 0)
    send = lax.dynamic_slice_in_dim(values, (1 - col) * share, share, 0)
    scores = keep + swap(send, "col", 1)

    total = None
    weight_grad = None
    for c in range(CHUNKS):
        weights = lax.slice_in_dim(down_weight, c * width, (c + 1) * width, axis=1)
        term = lax.dot_general(
            parts[c], weights, (((1,), (1,)), ((), ())), preferred_element_type=f32
        )
        total = term if total is None else total + term
        weight_grad = product_into(hidden_t, parts[c], weight_grad, c, CHUNKS)
    tokens = total.shape[0] // 2
    keep = lax.dynamic_slice_in_dim(total, col * tokens, tokens, 0)
    send = lax.dynamic_slice_in_dim(total, (1 - col) * tokens, tokens, 0)
    grad_hidden = (keep + swap(send, "col", 1)).astype(jnp.bfloat16)
    return (grad_hidden, weight_grad, scores)


def gather_kernel(
    n,
    g, hto, w, pin, pout, q, ids,
    G, ht, wgp, acc, rcv, wl, wx, gx, sc,
    wbuf, gown, pin_v, pout_v, q_v, ids_v, ofo, ofx, ifo, ifp, ift, ifx, ifs,
    pu, pd, pur, pdr, side_src, side, sidex, oft, idrow, qs, tbuf, pb, pbx,
    s_own, s_fz, s_fx, s_a, r_z, r_x, r_xo, r_a,
    t_own, t_fz, t_fx, u_z, u_x, u_xo,
    l_own, l_w, l_misc, c_send, c_recv, k_send, k_recv, g_send, g_recv,
):
    f32 = jnp.float32
    pieces, tokens, width = G.shape
    rows_of = tokens // n
    ff = ht.shape[0]
    half = tokens // 2
    quarter = width // 4
    nz = n // 2
    lag = nz - 1
    steps = pieces + lag - 1
    tile = ff // 2
    rank = pout_v.shape[0]
    hr = rank // 2
    early = wgp.shape[0]
    last = pieces - gx.shape[0]
    nq = q_v.shape[0]

    me = lax.axis_index("row")
    c = lax.axis_index("col")
    z, x = me // 2, me % 2
    has = (z < nz - 1, z > 0)
    nxt = ({"row": me + 2}, {"row": me - 2})
    xp = {"row": me + 1 - 2 * x}
    cp = {"col": 1 - c}

    def rc(src, dst, send, recv, dev):
        return pltpu.make_async_remote_copy(
            src_ref=src, dst_ref=dst, send_sem=send, recv_sem=recv, device_id=dev, device_id_type=MESH
        )

    def lc(src, dst, sem):
        return pltpu.make_async_copy(src, dst, sem)

    def rows(b):
        return pl.ds(pl.multiple_of(b * rows_of, 16), rows_of)

    def cols(s):
        return pl.ds(pl.multiple_of(s * width, 128), width)

    def at_z(d, h):
        return z - h if d == 0 else z + h

    def there(d, h):
        return z >= h if d == 0 else z + h < nz

    def own_z(d, s):
        return rc(g.at[:, cols(s)], G.at[s, rows(me)], s_own.at[d, s], r_z.at[d, 0, s], nxt[d])

    def own_x(s):
        return rc(g.at[:, cols(s)], G.at[s, rows(me)], s_own.at[2, s], r_xo.at[s], xp)

    def fwd_z(d, h, s):
        part = G.at[s, rows(at_z(d, h) * 2 + x)]
        return rc(part, part, s_fz.at[d, h - 1, s], r_z.at[d, h, s], nxt[d])

    def fwd_x(d, h, s, odd, other=False):
        xx = 1 - x if other else x
        r = rows(at_z(d, h) * 2 + xx)
        cut = quarter * (1 + odd)
        part = G.at[s, r, pl.ds(cut, width - cut)] if h == 1 else G.at[s, r]
        return rc(part, part, s_fx.at[d, h - 1, s], r_x.at[d, h - 1, s], xp)

    def fwd_a(d, s, odd):
        part = G.at[s, rows(z * 2 + 1 - x), pl.ds(0, quarter * (1 + odd))]
        return rc(part, part, s_a.at[d, s], r_a.at[d, s], nxt[d])

    def by_parity(s, f):
        for odd in (0, 1):
            @pl.when(lax.rem(s, 2) == odd)
            def _():
                f(odd)

    def got_z(d, h, s):
        part = G.at[s, rows(at_z(d, h) * 2 + x)]
        return rc(part, part, s_own.at[d, s], r_z.at[d, h - 1, s], nxt[d])

    def got_xo(s):
        part = G.at[s, rows(z * 2 + 1 - x)]
        return rc(part, part, s_own.at[2, s], r_xo.at[s], xp)

    def got_a(d, s, odd):
        part = G.at[s, rows(at_z(d, 1) * 2 + 1 - x), pl.ds(0, quarter * (1 + odd))]
        return rc(part, part, s_a.at[d, s], r_a.at[d, s], nxt[d])

    def t_own_z(d):
        return rc(side_src, side.at[me], t_own.at[d], u_z.at[d, 0], nxt[d])

    def t_own_x():
        return rc(side_src, side.at[me], t_own.at[2], u_xo.at[0], xp)

    def t_fwd_z(d, h):
        part = side.at[at_z(d, h) * 2 + x]
        return rc(part, part, t_fz.at[d, h - 1], u_z.at[d, h], nxt[d])

    def t_fwd_x(d, h, other=False):
        part = side.at[at_z(d, h) * 2 + (1 - x if other else x)]
        return rc(part, part, t_fx.at[d, h - 1], u_x.at[d, h - 1], xp)

    def t_got_z(d, h):
        part = side.at[at_z(d, h) * 2 + x]
        return rc(part, part, t_own.at[d], u_z.at[d, h - 1], nxt[d])

    def t_got_xo():
        part = side.at[z * 2 + 1 - x]
        return rc(part, part, t_own.at[2], u_xo.at[0], xp)

    def tok_half(ref, k):
        return ref.at[:, pl.ds(pl.multiple_of(k * half, 128), half)]

    def core_ht():
        return rc(hto, tok_half(ht, c), c_send.at[0], c_recv.at[0], cp)

    def core_wx():
        return rc(w.at[:, pl.ds(last * width, (pieces - last) * width)], wx, c_send.at[1], c_recv.at[1], cp)

    def core_of():
        return rc(ofo, ofx, c_send.at[2], c_recv.at[2], cp)

    def core_if():
        src = ifo.at[pl.ds(pl.multiple_of((1 - c) * hr, 8), hr)]
        return rc(src, tok_half(ifp, c), c_send.at[4], c_recv.at[4], cp)

    def core_side():
        return rc(side, sidex, c_send.at[3], c_recv.at[3], cp)

    def core_acc(k):
        r = pl.ds(k * tile, tile)
        return rc(acc.at[1 - c, r], rcv.at[r], k_send.at[3 + k], k_recv.at[3 + k], cp)

    def core_gx(s):
        src = G.at[s, pl.ds(pl.multiple_of((1 - c) * half, 16), half)]
        return rc(src, gx.at[s - last], g_send.at[s - last], g_recv.at[s - last], cp)

    def core_pb():
        share = nq // 2
        src = pb.at[pl.ds(pl.multiple_of((1 - c) * share, 8), share)]
        return rc(src, pbx, c_send.at[6], c_recv.at[6], cp)

    def x_half(ref, k):
        return ref.at[:, pl.ds(pl.multiple_of(k * half, 128), half)]

    def if_x():
        return rc(x_half(ifp, 1 - x), ifx, k_send.at[0], k_recv.at[0], xp)

    def if_back(other=False):
        part = x_half(ift, 1 - x if other else x)
        return rc(part, part, k_send.at[5], k_recv.at[5], xp)

    def if_up():
        return rc(pu, pur, k_send.at[1], k_recv.at[1], nxt[0])

    def if_dn():
        return rc(pd, pdr, k_send.at[2], k_recv.at[2], nxt[1])

    def load_own(s):
        return lc(g.at[:, cols(s)], G.at[s, rows(me)], l_own.at[s])

    def load_w(s, slot):
        return lc(w.at[:, cols(s)], wbuf.at[slot], l_w.at[slot])

    loads = (
        lambda: lc(g, gown, l_misc.at[0]),
        lambda: lc(pout, pout_v, l_misc.at[1]),
        lambda: lc(hto, tok_half(ht, c), l_misc.at[2]),
        lambda: lc(pin, pin_v, l_misc.at[3]),
        lambda: lc(q, q_v, l_misc.at[4]),
        lambda: lc(ids, ids_v, l_misc.at[5]),
        lambda: lc(w.at[:, pl.ds(last * width, (pieces - last) * width)], wl, l_misc.at[6]),
    )

    barrier = pltpu.get_barrier_semaphore()
    for d in (0, 1):
        @pl.when(has[d])
        def _():
            pl.semaphore_signal(barrier, inc=1, device_id=nxt[d], device_id_type=MESH)
    pl.semaphore_signal(barrier, inc=1, device_id=xp, device_id_type=MESH)
    pl.semaphore_signal(barrier, inc=1, device_id=cp, device_id_type=MESH)
    for k in (0, 1, 2, 3, 4, 5):
        loads[k]().start()
    for s in range(2):
        load_w(s, s).start()
    pur[...] = jnp.zeros_like(pur)
    pdr[...] = jnp.zeros_like(pdr)
    side_src[...] = jnp.zeros_like(side_src)
    acc[...] = jnp.zeros_like(acc)
    pl.semaphore_wait(barrier, 2 + jnp.where(has[0], 1, 0) + jnp.where(has[1], 1, 0))

    def send_own(s):
        for d in (0, 1):
            @pl.when(has[d])
            def _():
                own_z(d, s).start()
        own_x(s).start()
        load_own(s).start()

    for s in range(AHEAD):
        send_own(s)
    loads[6]().start()

    def hop(h, s):
        @pl.when((s >= 0) & (s < pieces))
        def _():
            for d in (0, 1):
                @pl.when(there(d, h))
                def _():
                    got_z(d, h, s).wait_recv()
                    if h < nz - 1:
                        @pl.when(has[d])
                        def _():
                            fwd_z(d, h, s).start()
                    if h == 1:
                        by_parity(s, lambda odd: fwd_x(d, h, s, odd).start())
                    else:
                        fwd_x(d, h, s, 0).start()

    def cross(s):
        @pl.when((s >= 0) & (s < pieces))
        def _():
            got_xo(s).wait_recv()
            for d in (0, 1):
                @pl.when(has[d])
                def _():
                    by_parity(s, lambda odd: fwd_a(d, s, odd).start())

    def finish(s):
        load_own(s).wait()
        for d in (0, 1):
            for h in range(1, nz):
                @pl.when(there(d, h))
                def _():
                    if h == 1:
                        def both(odd):
                            fwd_x(d, h, s, odd, True).wait_recv()
                            got_a(d, s, odd).wait_recv()

                        by_parity(s, both)
                    else:
                        fwd_x(d, h, s, 0, True).wait_recv()

    def side_hop(h, s):
        @pl.when(s == 2 + h)
        def _():
            for d in (0, 1):
                @pl.when(there(d, h))
                def _():
                    t_got_z(d, h).wait_recv()
                    if h < nz - 1:
                        @pl.when(has[d])
                        def _():
                            t_fwd_z(d, h).start()
                    t_fwd_x(d, h).start()

    def grads(s, slot, k):
        r = pl.ds(pl.multiple_of(k * tile, 16), tile)
        t = lax.dot_general(wbuf[slot, r, :], G[s], NT, preferred_element_type=f32)
        acc[0, r, :] += t[:, :half]
        acc[1, r, :] += t[:, half:]

    def weights(s, k):
        r = pl.ds(pl.multiple_of(k * tile, 16), tile)
        wgp[s, r, :] = jnp.dot(ht[r, :], G[s], preferred_element_type=f32).astype(wgp.dtype)

    def thirds(v):
        a = v.astype(jnp.bfloat16)
        rest = v - a.astype(f32)
        b = rest.astype(jnp.bfloat16)
        return a, b, (rest - b.astype(f32)).astype(jnp.bfloat16)

    def scores_part():
        hh = hr // 2
        core_side().wait_recv()
        if_back(True).wait_recv()
        mine = pl.multiple_of(c * hr, 8)
        others = pl.multiple_of((1 - c) * hr, 8)
        for b in range(n):
            t = slice(b * rows_of, (b + 1) * rows_of)
            for k in (0, 1):
                lanes = slice(k * rows_of, (k + 1) * rows_of)
                oft[pl.ds(mine + k * hh, hh), t] = side[b, 0:hh, lanes]
                oft[pl.ds(others + k * hh, hh), t] = sidex[b, 0:hh, lanes]
            idrow[0:1, t] = side[b, hh:hh + 1, 0:rows_of]
        tbuf[...] = jnp.dot(
            qs[...], jnp.concatenate(thirds(oft[...]), axis=0), preferred_element_type=f32
        )
        per = jnp.zeros((nq, tokens), f32)
        for i in range(hr):
            per = per + tbuf[i * nq:(i + 1) * nq, :] * ift[i:i + 1, :]
        labels = lax.broadcasted_iota(jnp.int32, (EXAMPLES, tokens), 0).astype(f32)
        mask = jnp.where(labels == idrow[...], 1.0, 0.0).astype(jnp.bfloat16)
        part = lax.dot_general(
            jnp.concatenate(thirds(per), axis=0), mask, NT, preferred_element_type=f32
        )
        pb[...] = jnp.zeros_like(pb)
        pb[:, 0:EXAMPLES] = part[:nq] + part[nq:2 * nq] + part[2 * nq:]

    def small_first(s):
        hh = hr // 2

        @pl.when(s == 0)
        def _():
            core_of().wait_recv()
            loads[5]().wait()
            mine = pl.ds(pl.multiple_of(c * hr, 8), hr)
            both = ofo[mine, :] + ofx[mine, :]
            side_src[0:hh, 0:rows_of] = both[:hh]
            side_src[0:hh, rows_of:2 * rows_of] = both[hh:]
            side_src[hh:hh + 1, 0:rows_of] = ids_v[...].astype(f32)
            core_if().wait_recv()
            ifp[:, pl.ds(pl.multiple_of(c * half, 128), half)] = ifo[mine, :]

        @pl.when(s == 2)
        def _():
            if_x().wait_recv()
            mine = pl.ds(pl.multiple_of(x * half, 128), half)
            ifs[...] = ifp[:, mine] + ifx[...]

        @pl.when((s == 3 + z) & has[0])
        def _():
            @pl.when(z > 0)
            def _():
                if_up().wait_recv()
            pu[...] = ifs[...] + pur[...]

        @pl.when((s == 2 + nz - z) & has[1])
        def _():
            @pl.when(z < nz - 1)
            def _():
                if_dn().wait_recv()
            pd[...] = ifs[...] + pdr[...]

        for h in range(1, nz):
            side_hop(h, s)

        @pl.when(s == 3 + nz)
        def _():
            lc(side_src, side.at[me], l_misc.at[7]).wait()
            t_got_xo().wait_recv()
            for d in (0, 1):
                for h in range(1, nz):
                    @pl.when(there(d, h))
                    def _():
                        t_fwd_x(d, h, True).wait_recv()
            core_side().start()

            @pl.when(z == nz - 1)
            def _():
                if_up().wait_recv()

            @pl.when(z == 0)
            def _():
                if_dn().wait_recv()
            mine = pl.ds(pl.multiple_of(x * half, 128), half)
            ift[:, mine] = ifs[...] + pur[...] + pdr[...]

    def small_last(s):
        @pl.when(s == 0)
        def _():
            core_ht().start()

        @pl.when(s == 3)
        def _():
            core_wx().start()

        @pl.when(s == 1)
        def _():
            for d in (0, 1):
                @pl.when(has[d])
                def _():
                    t_own_z(d).start()
            t_own_x().start()
            lc(side_src, side.at[me], l_misc.at[7]).start()
            if_x().start()

        @pl.when((s == 3 + z) & has[0])
        def _():
            if_up().start()

        @pl.when((s == 2 + nz - z) & has[1])
        def _():
            if_dn().start()

        @pl.when(s == 3 + nz)
        def _():
            if_back().start()

    def drain(s):
        for d in (0, 1):
            @pl.when(has[d])
            def _():
                own_z(d, s).wait_send()
                by_parity(s, lambda odd: fwd_a(d, s, odd).wait_send())
            for h in range(1, nz):
                @pl.when(there(d, h))
                def _():
                    if h < nz - 1:
                        @pl.when(has[d])
                        def _():
                            fwd_z(d, h, s).wait_send()
                    if h == 1:
                        by_parity(s, lambda odd: fwd_x(d, h, s, odd).wait_send())
                    else:
                        fwd_x(d, h, s, 0).wait_send()
        own_x(s).wait_send()

    def step(s, carry):
        cc = s - lag
        slot = lax.rem(jnp.maximum(cc, 0), 2)
        on = (cc >= 0) & (cc < last)

        @pl.when(cc == last)
        def _():
            core_acc(1).start()

        for h in range(nz - 1, 2, -1):
            hop(h, s - h + 1)

        @pl.when(cc >= 0)
        def _():
            finish(cc)

            @pl.when(cc >= last)
            def _():
                core_gx(cc).start()

        @pl.when(on)
        def _():
            load_w(cc, slot).wait()
            grads(cc, slot, 0)

        hop(2, s - 1)
        hop(1, s)

        @pl.when(s + AHEAD < pieces)
        def _():
            send_own(s + AHEAD)

        @pl.when(cc == last - 1)
        def _():
            core_acc(0).start()

        @pl.when(on)
        def _():
            grads(cc, slot, 1)

            @pl.when(cc + 2 < last)
            def _():
                load_w(cc + 2, slot).start()

        small_first(s)

        @pl.when(on & (cc < early))
        def _():
            @pl.when(cc == 0)
            def _():
                core_ht().wait_recv()
            weights(cc, 0)

        cross(s - 1)

        @pl.when(on & (cc < early))
        def _():
            weights(cc, 1)

        small_last(s)

        @pl.when(cc >= 2)
        def _():
            drain(cc - 2)
        return carry

    loads[0]().wait()
    loads[1]().wait()
    ofo[...] = lax.dot_general(pout_v[...], gown[...], NT, preferred_element_type=f32)
    loads[2]().wait()
    loads[3]().wait()
    ifo[...] = jnp.dot(
        pin_v[...], tok_half(ht, c)[...], preferred_element_type=f32
    )
    core_of().start()
    core_if().start()
    loads[4]().wait()
    for i in range(hr):
        for k in range(3):
            qs[i * nq:(i + 1) * nq, k * rank:(k + 1) * rank] = q_v[:, i * rank:(i + 1) * rank]

    lax.fori_loop(0, steps, step, 0)

    scores_part()
    core_pb().start()
    finish(pieces - 1)
    core_gx(pieces - 1).start()

    core_wx().wait()
    loads[6]().wait()
    core_ht().wait_send()
    core_of().wait_send()
    core_if().wait_send()
    core_side().wait_send()
    if_x().wait_send()
    if_back().wait_send()

    pl.loop(steps - lag - 2, pieces)(drain)
    for d in (0, 1):
        @pl.when(has[d])
        def _():
            t_own_z(d).wait_send()
            (if_up, if_dn)[d]().wait_send()
        for h in range(1, nz):
            @pl.when(there(d, h))
            def _():
                if h < nz - 1:
                    @pl.when(has[d])
                    def _():
                        t_fwd_z(d, h).wait_send()
                t_fwd_x(d, h).wait_send()
    t_own_x().wait_send()

    core_pb().wait()
    share = nq // 2
    sc[...] = pb[pl.ds(pl.multiple_of(c * share, 8), share), :] + pbx[...]
    for k in (0, 1):
        core_acc(k).wait()
    for s in range(last, pieces):
        core_gx(s).wait()


def finish_kernel(G, ht, wgp, acc, rcv, wl, wx, gx, sc, wg, gh, scores, stage, ghb, sems, gsem):
    f32 = jnp.float32
    pieces, tokens, width = G.shape
    ff = ht.shape[0]
    half = tokens // 2
    early = wgp.shape[0]
    tile = ff // 2
    c = lax.axis_index("col")

    def out(s, src):
        return pltpu.make_async_copy(src, wg.at[:, pl.ds(s * width, width)], sems.at[s])

    for s in range(early):
        out(s, wgp.at[s]).start()
    for s in range(early, pieces):
        @pl.loop(0, 2)
        def _(k):
            r = pl.ds(pl.multiple_of(k * tile, 16), tile)
            stage[s - early, r, :] = jnp.dot(
                ht[r, :], G[s], preferred_element_type=f32
            ).astype(stage.dtype)
        out(s, stage.at[s - early]).start()
    mine = pl.ds(pl.multiple_of(c * half, 16), half)
    part = ff // 4

    @pl.loop(0, 4)
    def _(k):
        r = pl.ds(pl.multiple_of(k * part, 16), part)
        t = acc[c, r, :] + rcv[r, :]
        for s in range(gx.shape[0]):
            at = pl.ds(s * width, width)
            own = G[pieces - gx.shape[0] + s, mine, :]
            t = t + lax.dot_general(wl[r, at], own, NT, preferred_element_type=f32)
            t = t + lax.dot_general(wx[r, at], gx[s], NT, preferred_element_type=f32)
        ghb[r, :] = t.astype(ghb.dtype)
        pltpu.make_async_copy(ghb.at[r], gh.at[r], gsem.at[k]).start()
    scores[...] = sc[:, 0:scores.shape[1]]
    for k in range(4):
        r = pl.ds(k * part, part)
        pltpu.make_async_copy(ghb.at[r], gh.at[r], gsem.at[k]).wait()
    for s in range(pieces):
        out(s, wgp.at[s] if s < early else stage.at[s - early]).wait()


def fused_body(grad_out, hidden_act, down_weight, proj_in, proj_out, queries, example_ids):
    bf16, f32, dma = jnp.bfloat16, jnp.float32, pltpu.SemaphoreType.DMA
    n = lax.axis_size("row")
    nz = n // 2
    rows_of, depth = grad_out.shape
    tokens = n * rows_of
    half, ff = hidden_act.shape
    width = depth // PIECES
    rank = proj_in.shape[1]
    hr = rank // 2
    nq = queries.shape[0]
    vm = pltpu.VMEM
    v_spec = pl.BlockSpec(memory_space=pltpu.VMEM)
    h_spec = pl.BlockSpec(memory_space=pltpu.HBM)

    args = (
        grad_out, hidden_act.T, down_weight, proj_in.T, proj_out.T, queries, example_ids.reshape(1, -1)
    )
    args = tuple(pltpu.with_memory_space_constraint(a, pltpu.HBM) for a in args)
    held = pl.pallas_call(
        functools.partial(gather_kernel, n),
        in_specs=[h_spec] * 7,
        out_specs=(v_spec,) * 9,
        out_shape=(
            vm((PIECES, tokens, width), bf16),
            vm((ff, tokens), bf16),
            vm((EARLY, ff, width), bf16),
            vm((2, ff, half), f32),
            vm((ff, half), f32),
            vm((ff, LATE * width), bf16),
            vm((ff, LATE * width), bf16),
            vm((LATE, half, width), bf16),
            vm((nq // 2, 128), f32),
        ),
        scratch_shapes=[
            vm((2, ff, width), bf16),
            vm((rows_of, depth), bf16),
            vm((rank, ff), bf16),
            vm((rank, depth), bf16),
            vm((nq, hr * rank), bf16),
            vm((1, rows_of), jnp.int32),
            vm((rank, rows_of), f32),
            vm((rank, rows_of), f32),
            vm((rank, half), f32),
        ] + [vm((hr, tokens), f32)] * 2 + [vm((hr, half), f32)] * 6 + [
            vm((hr // 2 + 1, 2 * rows_of), f32),
            vm((n, hr // 2 + 1, 2 * rows_of), f32),
            vm((n, hr // 2 + 1, 2 * rows_of), f32),
            vm((rank, tokens), f32),
            vm((1, tokens), f32),
            vm((hr * nq, 3 * rank), bf16),
            vm((hr * nq, tokens), f32),
            vm((nq, 128), f32),
            vm((nq // 2, 128), f32),
            dma((3, PIECES)),
            dma((2, nz - 2, PIECES)),
            dma((2, nz - 1, PIECES)),
            dma((2, PIECES)),
            dma((2, nz - 1, PIECES)),
            dma((2, nz - 1, PIECES)),
            dma((PIECES,)),
            dma((2, PIECES)),
            dma((3,)),
            dma((2, nz - 2)),
            dma((2, nz - 1)),
            dma((2, nz - 1)),
            dma((2, nz - 1)),
            dma((1,)),
            dma((PIECES,)),
            dma((2,)),
            dma((8,)),
            dma((7,)),
            dma((7,)),
            dma((6,)),
            dma((6,)),
            dma((LATE,)),
            dma((LATE,)),
        ],
        compiler_params=pltpu.CompilerParams(
            collective_id=0, has_side_effects=True, vmem_limit_bytes=11 << 20
        ),
    )(*args)

    wg, gh, scores = pl.pallas_call(
        finish_kernel,
        in_specs=[v_spec] * 9,
        out_specs=(h_spec, h_spec, v_spec),
        out_shape=(
            jax.ShapeDtypeStruct((ff, depth), bf16),
            jax.ShapeDtypeStruct((ff, half), bf16),
            jax.ShapeDtypeStruct((nq // 2, EXAMPLES), f32),
        ),
        scratch_shapes=[
            vm((PIECES - EARLY, ff, width), bf16),
            vm((ff, half), bf16),
            dma((PIECES,)),
            dma((4,)),
        ],
        compiler_params=pltpu.CompilerParams(vmem_limit_bytes=11 << 20),
    )(*held)
    return (gh.T, wg, scores)


def fits(mesh, shapes):
    n = mesh.shape["row"]
    if mesh.shape["col"] != 2 or n % 2 or not 6 <= n <= 16 or PIECES < n // 2 + 4:
        return False
    grad_out, hidden_act, _, proj_in, _, queries, _ = shapes
    parts = mesh.shape["grp"]
    rows_of = grad_out[0] // (parts * n)
    ff = hidden_act[1] // n
    rank = proj_in[1]
    return (
        2 * rows_of == 128
        and grad_out[1] % (2 * PIECES * 256) == 0
        and ff % 64 == 0
        and rank % 32 == 0
        and queries[0] % (16 * n) == 0
        and queries[1] == rank * rank
        and ff * (rows_of * n + grad_out[1]) < 24 << 20
    )


def solution(mesh):
    def run(*args):
        body = fused_body if fits(mesh, [a.shape for a in args]) else plain_body
        return jax.shard_map(
            body,
            mesh=mesh,
            in_specs=(
                P(("grp", "row"), "col"),
                P(("grp", "col"), "row"),
                P("row", "col"),
                P("row", None),
                P("col", None),
                P("row", "col"),
                P(("grp", "row")),
            ),
            out_specs=(P(("grp", "col"), "row"), P(("grp", "row"), "col"), P(("row", "col"), "grp")),
            check_vma=False,
        )(*args)

    return run
```

```python
import functools

import jax
import jax.numpy as jnp
from jax import lax
from jax.experimental import pallas as pl
from jax.experimental.pallas import tpu as pltpu
from jax.sharding import PartitionSpec as P

EXAMPLES = 8
CHUNKS = 4
PIECES = 8
AHEAD = 3
EARLY = 6
LATE = 2

MESH = pl.DeviceIdType.MESH
NT = (((1,), (1,)), ((), ()))


def swap(x, axis, bit):
    n = lax.axis_size(axis)
    return lax.ppermute(x, axis, [(i, i ^ bit) for i in range(n)])


def pair_order(own, other, index, axis):
    first = jnp.where(index == 0, own, other)
    second = jnp.where(index == 0, other, own)
    return jnp.concatenate([first, second], axis=axis)


def gather_rows(block):
    n = lax.axis_size("row")
    if n % 2 or n > 16:
        return lax.all_gather(block, "row", axis=0, tiled=True)
    outer = n // 2
    me = lax.axis_index("row")
    z, x = me // 2, me % 2
    held = [block]
    for k in range(1, outer):
        perm = [(i, ((i // 2 + k) % outer) * 2 + i % 2) for i in range(n)]
        held.append(lax.ppermute(block, "row", perm))
    mine = jnp.stack(held[::-1])
    theirs = swap(mine, "row", 1)
    both = pair_order(mine, theirs, x, 1)
    twice = jnp.concatenate([both, both], axis=0)
    rows = lax.dynamic_slice_in_dim(twice, outer - 1 - z, outer, 0)
    return rows.reshape((n * block.shape[0],) + block.shape[1:])


def sum_rows(x):
    n = lax.axis_size("row")
    if n & (n - 1):
        return lax.psum(x, "row")
    bit = 1
    while bit < n:
        x = x + swap(x, "row", bit)
        bit *= 2
    return x


def product_kernel(a_ref, b_ref, *refs):
    out_ref = refs[-1]
    out_ref[...] = jnp.dot(
        a_ref[...], b_ref[...], preferred_element_type=jnp.float32
    ).astype(out_ref.dtype)


def product_into(a, b, total, at, chunks):
    rows, depth = a.shape
    width = b.shape[1]
    tile = rows
    for parts in (8, 4, 2):
        if rows % (parts * 16) == 0:
            tile = rows // parts
            break
    in_specs = [
        pl.BlockSpec((tile, depth), lambda i: (i, 0)),
        pl.BlockSpec((depth, width), lambda i: (0, 0)),
    ]
    args = (a, b)
    aliases = {}
    if total is not None:
        in_specs.append(pl.BlockSpec(memory_space=pl.ANY))
        args = (a, b, total)
        aliases = {2: 0}
    return pl.pallas_call(
        product_kernel,
        grid=(rows // tile,),
        in_specs=in_specs,
        out_specs=pl.BlockSpec((tile, width), lambda i: (i, at)),
        out_shape=jax.ShapeDtypeStruct((rows, chunks * width), jnp.bfloat16),
        input_output_aliases=aliases,
        compiler_params=pltpu.CompilerParams(vmem_limit_bytes=24 << 20),
        cost_estimate=pl.CostEstimate(
            flops=2 * rows * depth * width,
            bytes_accessed=2 * (rows * depth + depth * width + rows * width),
            transcendentals=0,
        ),
    )(*args)


def plain_body(grad_out, hidden_act, down_weight, proj_in, proj_out, queries, example_ids):
    f32 = jnp.float32
    col = lax.axis_index("col")
    half_rank = proj_in.shape[1] // lax.axis_size("col")

    width = grad_out.shape[1] // CHUNKS
    parts = [
        gather_rows(lax.slice_in_dim(grad_out, c * width, (c + 1) * width, axis=1))
        for c in range(CHUNKS)
    ]

    other_hidden = swap(hidden_act, "col", 1)
    full_hidden = pair_order(hidden_act, other_hidden, col, 0)
    hidden_t = full_hidden.T

    own_proj = lax.dynamic_slice_in_dim(proj_in, col * half_rank, half_rank, 1)
    in_factor = sum_rows(
        lax.dot_general(own_proj, full_hidden, (((0,), (1,)), ((), ())), preferred_element_type=f32)
    )

    out_own = lax.dot_general(
        proj_out, grad_out, (((0,), (1,)), ((), ())), preferred_element_type=f32
    ).T
    out_own = out_own + swap(out_own, "col", 1)
    packed = gather_rows(jnp.concatenate([out_own, example_ids[:, None].astype(f32)], axis=1))
    out_factor = packed[:, :-1]
    ids = packed[:, -1].astype(jnp.int32)
    labels = jnp.arange(EXAMPLES, dtype=jnp.int32)
    onehot = ids[None, :] == labels[:, None]
    masked = jnp.where(onehot[:, None, :], in_factor[None], 0.0)
    example_grads = jnp.dot(
        masked.reshape(EXAMPLES * half_rank, -1), out_factor, precision=lax.Precision.HIGHEST
    ).reshape(EXAMPLES, -1)
    values = lax.dot_general(
        queries.astype(f32), example_grads, (((1,), (1,)), ((), ())), precision=lax.Precision.HIGHEST
    )
    share = values.shape[0] // 2
    keep = lax.dynamic_slice_in_dim(values, col * share, share, 0)
    send = lax.dynamic_slice_in_dim(values, (1 - col) * share, share, 0)
    scores = keep + swap(send, "col", 1)

    total = None
    weight_grad = None
    for c in range(CHUNKS):
        weights = lax.slice_in_dim(down_weight, c * width, (c + 1) * width, axis=1)
        term = lax.dot_general(
            parts[c], weights, (((1,), (1,)), ((), ())), preferred_element_type=f32
        )
        total = term if total is None else total + term
        weight_grad = product_into(hidden_t, parts[c], weight_grad, c, CHUNKS)
    tokens = total.shape[0] // 2
    keep = lax.dynamic_slice_in_dim(total, col * tokens, tokens, 0)
    send = lax.dynamic_slice_in_dim(total, (1 - col) * tokens, tokens, 0)
    grad_hidden = (keep + swap(send, "col", 1)).astype(jnp.bfloat16)
    return (grad_hidden, weight_grad, scores)


def gather_kernel(
    n,
    g, hto, w, pin, pout, q, ids,
    G, ht, wgp, acc, rcv, wl, wx, gx, sc,
    wbuf, gown, pin_v, pout_v, q_v, ids_v, ofo, ofx, ifo, ifp, ift, ifx, ifs,
    pu, pd, pur, pdr, side_src, side, sidex, oft, idrow, qs, tbuf, pb, pbx,
    s_own, s_fz, s_fx, s_a, r_z, r_x, r_xo, r_a,
    t_own, t_fz, t_fx, u_z, u_x, u_xo,
    l_own, l_w, l_misc, c_send, c_recv, k_send, k_recv, g_send, g_recv,
):
    f32 = jnp.float32
    pieces, tokens, width = G.shape
    rows_of = tokens // n
    ff = ht.shape[0]
    half = tokens // 2
    quarter = width // 4
    nz = n // 2
    lag = nz - 1
    steps = pieces + lag - 1
    tile = ff // 2
    rank = pout_v.shape[0]
    hr = rank // 2
    early = wgp.shape[0]
    last = pieces - gx.shape[0]
    nq = q_v.shape[0]

    me = lax.axis_index("row")
    c = lax.axis_index("col")
    z, x = me // 2, me % 2
    has = (z < nz - 1, z > 0)
    nxt = ({"row": me + 2}, {"row": me - 2})
    xp = {"row": me + 1 - 2 * x}
    cp = {"col": 1 - c}

    def rc(src, dst, send, recv, dev):
        return pltpu.make_async_remote_copy(
            src_ref=src, dst_ref=dst, send_sem=send, recv_sem=recv, device_id=dev, device_id_type=MESH
        )

    def lc(src, dst, sem):
        return pltpu.make_async_copy(src, dst, sem)

    def rows(b):
        return pl.ds(pl.multiple_of(b * rows_of, 16), rows_of)

    def cols(s):
        return pl.ds(pl.multiple_of(s * width, 128), width)

    def at_z(d, h):
        return z - h if d == 0 else z + h

    def there(d, h):
        return z >= h if d == 0 else z + h < nz

    def own_z(d, s):
        return rc(g.at[:, cols(s)], G.at[s, rows(me)], s_own.at[d, s], r_z.at[d, 0, s], nxt[d])

    def own_x(s):
        return rc(g.at[:, cols(s)], G.at[s, rows(me)], s_own.at[2, s], r_xo.at[s], xp)

    def fwd_z(d, h, s):
        part = G.at[s, rows(at_z(d, h) * 2 + x)]
        return rc(part, part, s_fz.at[d, h - 1, s], r_z.at[d, h, s], nxt[d])

    def fwd_x(d, h, s, odd, other=False):
        xx = 1 - x if other else x
        r = rows(at_z(d, h) * 2 + xx)
        cut = quarter * (1 + odd)
        part = G.at[s, r, pl.ds(cut, width - cut)] if h == 1 else G.at[s, r]
        return rc(part, part, s_fx.at[d, h - 1, s], r_x.at[d, h - 1, s], xp)

    def fwd_a(d, s, odd):
        part = G.at[s, rows(z * 2 + 1 - x), pl.ds(0, quarter * (1 + odd))]
        return rc(part, part, s_a.at[d, s], r_a.at[d, s], nxt[d])

    def by_parity(s, f):
        for odd in (0, 1):
            @pl.when(lax.rem(s, 2) == odd)
            def _():
                f(odd)

    def got_z(d, h, s):
        part = G.at[s, rows(at_z(d, h) * 2 + x)]
        return rc(part, part, s_own.at[d, s], r_z.at[d, h - 1, s], nxt[d])

    def got_xo(s):
        part = G.at[s, rows(z * 2 + 1 - x)]
        return rc(part, part, s_own.at[2, s], r_xo.at[s], xp)

    def got_a(d, s, odd):
        part = G.at[s, rows(at_z(d, 1) * 2 + 1 - x), pl.ds(0, quarter * (1 + odd))]
        return rc(part, part, s_a.at[d, s], r_a.at[d, s], nxt[d])

    def t_own_z(d):
        return rc(side_src, side.at[me], t_own.at[d], u_z.at[d, 0], nxt[d])

    def t_own_x():
        return rc(side_src, side.at[me], t_own.at[2], u_xo.at[0], xp)

    def t_fwd_z(d, h):
        part = side.at[at_z(d, h) * 2 + x]
        return rc(part, part, t_fz.at[d, h - 1], u_z.at[d, h], nxt[d])

    def t_fwd_x(d, h, other=False):
        part = side.at[at_z(d, h) * 2 + (1 - x if other else x)]
        return rc(part, part, t_fx.at[d, h - 1], u_x.at[d, h - 1], xp)

    def t_got_z(d, h):
        part = side.at[at_z(d, h) * 2 + x]
        return rc(part, part, t_own.at[d], u_z.at[d, h - 1], nxt[d])

    def t_got_xo():
        part = side.at[z * 2 + 1 - x]
        return rc(part, part, t_own.at[2], u_xo.at[0], xp)

    def tok_half(ref, k):
        return ref.at[:, pl.ds(pl.multiple_of(k * half, 128), half)]

    def core_ht():
        return rc(hto, tok_half(ht, c), c_send.at[0], c_recv.at[0], cp)

    def core_wx():
        return rc(w.at[:, pl.ds(last * width, (pieces - last) * width)], wx, c_send.at[1], c_recv.at[1], cp)

    def core_of():
        return rc(ofo, ofx, c_send.at[2], c_recv.at[2], cp)

    def core_if():
        src = ifo.at[pl.ds(pl.multiple_of((1 - c) * hr, 8), hr)]
        return rc(src, tok_half(ifp, c), c_send.at[4], c_recv.at[4], cp)

    def core_side():
        return rc(side, sidex, c_send.at[3], c_recv.at[3], cp)

    def core_acc(k):
        r = pl.ds(k * tile, tile)
        return rc(acc.at[1 - c, r], rcv.at[r], k_send.at[3 + k], k_recv.at[3 + k], cp)

    def core_gx(s):
        src = G.at[s, pl.ds(pl.multiple_of((1 - c) * half, 16), half)]
        return rc(src, gx.at[s - last], g_send.at[s - last], g_recv.at[s - last], cp)

    def core_pb():
        share = nq // 2
        src = pb.at[pl.ds(pl.multiple_of((1 - c) * share, 8), share)]
        return rc(src, pbx, c_send.at[6], c_recv.at[6], cp)

    def x_half(ref, k):
        return ref.at[:, pl.ds(pl.multiple_of(k * half, 128), half)]

    def if_x():
        return rc(x_half(ifp, 1 - x), ifx, k_send.at[0], k_recv.at[0], xp)

    def if_back(other=False):
        part = x_half(ift, 1 - x if other else x)
        return rc(part, part, k_send.at[5], k_recv.at[5], xp)

    def if_up():
        return rc(pu, pur, k_send.at[1], k_recv.at[1], nxt[0])

    def if_dn():
        return rc(pd, pdr, k_send.at[2], k_recv.at[2], nxt[1])

    def load_own(s):
        return lc(g.at[:, cols(s)], G.at[s, rows(me)], l_own.at[s])

    def load_w(s, slot):
        return lc(w.at[:, cols(s)], wbuf.at[slot], l_w.at[slot])

    loads = (
        lambda: lc(g, gown, l_misc.at[0]),
        lambda: lc(pout, pout_v, l_misc.at[1]),
        lambda: lc(hto, tok_half(ht, c), l_misc.at[2]),
        lambda: lc(pin, pin_v, l_misc.at[3]),
        lambda: lc(q, q_v, l_misc.at[4]),
        lambda: lc(ids, ids_v, l_misc.at[5]),
        lambda: lc(w.at[:, pl.ds(last * width, (pieces - last) * width)], wl, l_misc.at[6]),
    )

    barrier = pltpu.get_barrier_semaphore()
    for d in (0, 1):
        @pl.when(has[d])
        def _():
            pl.semaphore_signal(barrier, inc=1, device_id=nxt[d], device_id_type=MESH)
    pl.semaphore_signal(barrier, inc=1, device_id=xp, device_id_type=MESH)
    pl.semaphore_signal(barrier, inc=1, device_id=cp, device_id_type=MESH)
    for k in (0, 1, 2, 3, 4, 5):
        loads[k]().start()
    for s in range(2):
        load_w(s, s).start()
    pur[...] = jnp.zeros_like(pur)
    pdr[...] = jnp.zeros_like(pdr)
    side_src[...] = jnp.zeros_like(side_src)
    pl.semaphore_wait(barrier, 2 + jnp.where(has[0], 1, 0) + jnp.where(has[1], 1, 0))

    def send_own(s):
        for d in (0, 1):
            @pl.when(has[d])
            def _():
                own_z(d, s).start()
        own_x(s).start()
        load_own(s).start()

    for s in range(AHEAD):
        send_own(s)
    loads[6]().start()

    def hop(h, s):
        @pl.when((s >= 0) & (s < pieces))
        def _():
            for d in (0, 1):
                @pl.when(there(d, h))
                def _():
                    got_z(d, h, s).wait_recv()
                    if h < nz - 1:
                        @pl.when(has[d])
                        def _():
                            fwd_z(d, h, s).start()
                    if h == 1:
                        by_parity(s, lambda odd: fwd_x(d, h, s, odd).start())
                    else:
                        fwd_x(d, h, s, 0).start()

    def cross(s):
        @pl.when((s >= 0) & (s < pieces))
        def _():
            got_xo(s).wait_recv()
            for d in (0, 1):
                @pl.when(has[d])
                def _():
                    by_parity(s, lambda odd: fwd_a(d, s, odd).start())

    def finish(s):
        load_own(s).wait()
        for d in (0, 1):
            for h in range(1, nz):
                @pl.when(there(d, h))
                def _():
                    if h == 1:
                        def both(odd):
                            fwd_x(d, h, s, odd, True).wait_recv()
                            got_a(d, s, odd).wait_recv()

                        by_parity(s, both)
                    else:
                        fwd_x(d, h, s, 0, True).wait_recv()

    def side_hop(h, s):
        @pl.when(s == 2 + h)
        def _():
            for d in (0, 1):
                @pl.when(there(d, h))
                def _():
                    t_got_z(d, h).wait_recv()
                    if h < nz - 1:
                        @pl.when(has[d])
                        def _():
                            t_fwd_z(d, h).start()
                    t_fwd_x(d, h).start()

    def grads(s, slot, k):
        r = pl.ds(pl.multiple_of(k * tile, 16), tile)
        t = lax.dot_general(wbuf[slot, r, :], G[s], NT, preferred_element_type=f32)
        acc[0, r, :] += t[:, :half]
        acc[1, r, :] += t[:, half:]

    def weights(s, k):
        r = pl.ds(pl.multiple_of(k * tile, 16), tile)
        wgp[s, r, :] = jnp.dot(ht[r, :], G[s], preferred_element_type=f32).astype(wgp.dtype)

    def thirds(v):
        a = v.astype(jnp.bfloat16)
        rest = v - a.astype(f32)
        b = rest.astype(jnp.bfloat16)
        return a, b, (rest - b.astype(f32)).astype(jnp.bfloat16)

    def scores_part():
        hh = hr // 2
        core_side().wait_recv()
        if_back(True).wait_recv()
        mine = pl.multiple_of(c * hr, 8)
        others = pl.multiple_of((1 - c) * hr, 8)
        for b in range(n):
            t = slice(b * rows_of, (b + 1) * rows_of)
            for k in (0, 1):
                lanes = slice(k * rows_of, (k + 1) * rows_of)
                oft[pl.ds(mine + k * hh, hh), t] = side[b, 0:hh, lanes]
                oft[pl.ds(others + k * hh, hh), t] = sidex[b, 0:hh, lanes]
            idrow[0:1, t] = side[b, hh:hh + 1, 0:rows_of]
        tbuf[...] = jnp.dot(
            qs[...], jnp.concatenate(thirds(oft[...]), axis=0), preferred_element_type=f32
        )
        per = jnp.zeros((nq, tokens), f32)
        for i in range(hr):
            per = per + tbuf[i * nq:(i + 1) * nq, :] * ift[i:i + 1, :]
        labels = lax.broadcasted_iota(jnp.int32, (EXAMPLES, tokens), 0).astype(f32)
        mask = jnp.where(labels == idrow[...], 1.0, 0.0).astype(jnp.bfloat16)
        part = lax.dot_general(
            jnp.concatenate(thirds(per), axis=0), mask, NT, preferred_element_type=f32
        )
        pb[...] = jnp.zeros_like(pb)
        pb[:, 0:EXAMPLES] = part[:nq] + part[nq:2 * nq] + part[2 * nq:]

    def small_first(s):
        hh = hr // 2

        @pl.when(s == 0)
        def _():
            core_of().wait_recv()
            loads[5]().wait()
            mine = pl.ds(pl.multiple_of(c * hr, 8), hr)
            both = ofo[mine, :] + ofx[mine, :]
            side_src[0:hh, 0:rows_of] = both[:hh]
            side_src[0:hh, rows_of:2 * rows_of] = both[hh:]
            side_src[hh:hh + 1, 0:rows_of] = ids_v[...].astype(f32)
            core_if().wait_recv()
            ifp[:, pl.ds(pl.multiple_of(c * half, 128), half)] = ifo[mine, :]

        @pl.when(s == 2)
        def _():
            if_x().wait_recv()
            mine = pl.ds(pl.multiple_of(x * half, 128), half)
            ifs[...] = ifp[:, mine] + ifx[...]

        @pl.when((s == 3 + z) & has[0])
        def _():
            @pl.when(z > 0)
            def _():
                if_up().wait_recv()
            pu[...] = ifs[...] + pur[...]

        @pl.when((s == 2 + nz - z) & has[1])
        def _():
            @pl.when(z < nz - 1)
            def _():
                if_dn().wait_recv()
            pd[...] = ifs[...] + pdr[...]

        for h in range(1, nz):
            side_hop(h, s)

        @pl.when(s == 3 + nz)
        def _():
            lc(side_src, side.at[me], l_misc.at[7]).wait()
            t_got_xo().wait_recv()
            for d in (0, 1):
                for h in range(1, nz):
                    @pl.when(there(d, h))
                    def _():
                        t_fwd_x(d, h, True).wait_recv()
            core_side().start()

            @pl.when(z == nz - 1)
            def _():
                if_up().wait_recv()

            @pl.when(z == 0)
            def _():
                if_dn().wait_recv()
            mine = pl.ds(pl.multiple_of(x * half, 128), half)
            ift[:, mine] = ifs[...] + pur[...] + pdr[...]

    def small_last(s):
        @pl.when(s == 0)
        def _():
            core_ht().start()

        @pl.when(s == 3)
        def _():
            core_wx().start()

        @pl.when(s == 1)
        def _():
            for d in (0, 1):
                @pl.when(has[d])
                def _():
                    t_own_z(d).start()
            t_own_x().start()
            lc(side_src, side.at[me], l_misc.at[7]).start()
            if_x().start()

        @pl.when((s == 3 + z) & has[0])
        def _():
            if_up().start()

        @pl.when((s == 2 + nz - z) & has[1])
        def _():
            if_dn().start()

        @pl.when(s == 3 + nz)
        def _():
            if_back().start()

    def drain(s):
        for d in (0, 1):
            @pl.when(has[d])
            def _():
                own_z(d, s).wait_send()
                by_parity(s, lambda odd: fwd_a(d, s, odd).wait_send())
            for h in range(1, nz):
                @pl.when(there(d, h))
                def _():
                    if h < nz - 1:
                        @pl.when(has[d])
                        def _():
                            fwd_z(d, h, s).wait_send()
                    if h == 1:
                        by_parity(s, lambda odd: fwd_x(d, h, s, odd).wait_send())
                    else:
                        fwd_x(d, h, s, 0).wait_send()
        own_x(s).wait_send()

    def step(s, carry):
        cc = s - lag
        slot = lax.rem(jnp.maximum(cc, 0), 2)
        on = (cc >= 0) & (cc < last)

        @pl.when(cc == last)
        def _():
            core_acc(1).start()

        for h in range(nz - 1, 2, -1):
            hop(h, s - h + 1)

        @pl.when(cc >= 0)
        def _():
            finish(cc)

            @pl.when(cc >= last)
            def _():
                core_gx(cc).start()

        @pl.when(on)
        def _():
            load_w(cc, slot).wait()
            grads(cc, slot, 0)

        hop(2, s - 1)
        hop(1, s)

        @pl.when(s + AHEAD < pieces)
        def _():
            send_own(s + AHEAD)

        @pl.when(cc == last - 1)
        def _():
            core_acc(0).start()

        @pl.when(on)
        def _():
            grads(cc, slot, 1)

            @pl.when(cc + 2 < last)
            def _():
                load_w(cc + 2, slot).start()

        small_first(s)

        @pl.when(on & (cc < early))
        def _():
            @pl.when(cc == 0)
            def _():
                core_ht().wait_recv()
            weights(cc, 0)

        cross(s - 1)

        @pl.when(on & (cc < early))
        def _():
            weights(cc, 1)

        small_last(s)

        @pl.when(cc >= 2)
        def _():
            drain(cc - 2)
        return carry

    loads[0]().wait()
    loads[1]().wait()
    ofo[...] = lax.dot_general(pout_v[...], gown[...], NT, preferred_element_type=f32)
    loads[2]().wait()
    loads[3]().wait()
    ifo[...] = jnp.dot(
        pin_v[...], tok_half(ht, c)[...], preferred_element_type=f32
    )
    core_of().start()
    core_if().start()
    acc[...] = jnp.zeros_like(acc)
    loads[4]().wait()
    for i in range(hr):
        for k in range(3):
            qs[i * nq:(i + 1) * nq, k * rank:(k + 1) * rank] = q_v[:, i * rank:(i + 1) * rank]

    lax.fori_loop(0, steps, step, 0)

    scores_part()
    core_pb().start()
    finish(pieces - 1)
    core_gx(pieces - 1).start()

    core_wx().wait()
    loads[6]().wait()
    core_ht().wait_send()
    core_of().wait_send()
    core_if().wait_send()
    core_side().wait_send()
    if_x().wait_send()
    if_back().wait_send()

    pl.loop(steps - lag - 2, pieces)(drain)
    for d in (0, 1):
        @pl.when(has[d])
        def _():
            t_own_z(d).wait_send()
            (if_up, if_dn)[d]().wait_send()
        for h in range(1, nz):
            @pl.when(there(d, h))
            def _():
                if h < nz - 1:
                    @pl.when(has[d])
                    def _():
                        t_fwd_z(d, h).wait_send()
                t_fwd_x(d, h).wait_send()
    t_own_x().wait_send()

    core_pb().wait()
    share = nq // 2
    sc[...] = pb[pl.ds(pl.multiple_of(c * share, 8), share), :] + pbx[...]
    for k in (0, 1):
        core_acc(k).wait()
    for s in range(last, pieces):
        core_gx(s).wait()


def finish_kernel(G, ht, wgp, acc, rcv, wl, wx, gx, sc, wg, gh, scores, stage, ghb, sems, gsem):
    f32 = jnp.float32
    pieces, tokens, width = G.shape
    ff = ht.shape[0]
    half = tokens // 2
    early = wgp.shape[0]
    tile = ff // 2
    c = lax.axis_index("col")

    def out(s, src):
        return pltpu.make_async_copy(src, wg.at[:, pl.ds(s * width, width)], sems.at[s])

    for s in range(early):
        out(s, wgp.at[s]).start()
    for s in range(early, pieces):
        @pl.loop(0, 2)
        def _(k):
            r = pl.ds(pl.multiple_of(k * tile, 16), tile)
            stage[s - early, r, :] = jnp.dot(
                ht[r, :], G[s], preferred_element_type=f32
            ).astype(stage.dtype)
        out(s, stage.at[s - early]).start()
    mine = pl.ds(pl.multiple_of(c * half, 16), half)
    part = ff // 4

    @pl.loop(0, 4)
    def _(k):
        r = pl.ds(pl.multiple_of(k * part, 16), part)
        t = acc[c, r, :] + rcv[r, :]
        for s in range(gx.shape[0]):
            at = pl.ds(s * width, width)
            own = G[pieces - gx.shape[0] + s, mine, :]
            t = t + lax.dot_general(wl[r, at], own, NT, preferred_element_type=f32)
            t = t + lax.dot_general(wx[r, at], gx[s], NT, preferred_element_type=f32)
        ghb[r, :] = t.astype(ghb.dtype)
        pltpu.make_async_copy(ghb.at[r], gh.at[r], gsem.at[k]).start()
    scores[...] = sc[:, 0:scores.shape[1]]
    for k in range(4):
        r = pl.ds(k * part, part)
        pltpu.make_async_copy(ghb.at[r], gh.at[r], gsem.at[k]).wait()
    for s in range(pieces):
        out(s, wgp.at[s] if s < early else stage.at[s - early]).wait()


def fused_body(grad_out, hidden_act, down_weight, proj_in, proj_out, queries, example_ids):
    bf16, f32, dma = jnp.bfloat16, jnp.float32, pltpu.SemaphoreType.DMA
    n = lax.axis_size("row")
    nz = n // 2
    rows_of, depth = grad_out.shape
    tokens = n * rows_of
    half, ff = hidden_act.shape
    width = depth // PIECES
    rank = proj_in.shape[1]
    hr = rank // 2
    nq = queries.shape[0]
    vm = pltpu.VMEM
    v_spec = pl.BlockSpec(memory_space=pltpu.VMEM)
    h_spec = pl.BlockSpec(memory_space=pltpu.HBM)

    args = (
        grad_out, hidden_act.T, down_weight, proj_in.T, proj_out.T, queries, example_ids.reshape(1, -1)
    )
    args = tuple(pltpu.with_memory_space_constraint(a, pltpu.HBM) for a in args)
    held = pl.pallas_call(
        functools.partial(gather_kernel, n),
        in_specs=[h_spec] * 7,
        out_specs=(v_spec,) * 9,
        out_shape=(
            vm((PIECES, tokens, width), bf16),
            vm((ff, tokens), bf16),
            vm((EARLY, ff, width), bf16),
            vm((2, ff, half), f32),
            vm((ff, half), f32),
            vm((ff, LATE * width), bf16),
            vm((ff, LATE * width), bf16),
            vm((LATE, half, width), bf16),
            vm((nq // 2, 128), f32),
        ),
        scratch_shapes=[
            vm((2, ff, width), bf16),
            vm((rows_of, depth), bf16),
            vm((rank, ff), bf16),
            vm((rank, depth), bf16),
            vm((nq, hr * rank), bf16),
            vm((1, rows_of), jnp.int32),
            vm((rank, rows_of), f32),
            vm((rank, rows_of), f32),
            vm((rank, half), f32),
        ] + [vm((hr, tokens), f32)] * 2 + [vm((hr, half), f32)] * 6 + [
            vm((hr // 2 + 1, 2 * rows_of), f32),
            vm((n, hr // 2 + 1, 2 * rows_of), f32),
            vm((n, hr // 2 + 1, 2 * rows_of), f32),
            vm((rank, tokens), f32),
            vm((1, tokens), f32),
            vm((hr * nq, 3 * rank), bf16),
            vm((hr * nq, tokens), f32),
            vm((nq, 128), f32),
            vm((nq // 2, 128), f32),
            dma((3, PIECES)),
            dma((2, nz - 2, PIECES)),
            dma((2, nz - 1, PIECES)),
            dma((2, PIECES)),
            dma((2, nz - 1, PIECES)),
            dma((2, nz - 1, PIECES)),
            dma((PIECES,)),
            dma((2, PIECES)),
            dma((3,)),
            dma((2, nz - 2)),
            dma((2, nz - 1)),
            dma((2, nz - 1)),
            dma((2, nz - 1)),
            dma((1,)),
            dma((PIECES,)),
            dma((2,)),
            dma((8,)),
            dma((7,)),
            dma((7,)),
            dma((6,)),
            dma((6,)),
            dma((LATE,)),
            dma((LATE,)),
        ],
        compiler_params=pltpu.CompilerParams(
            collective_id=0, has_side_effects=True, vmem_limit_bytes=11 << 20
        ),
    )(*args)

    wg, gh, scores = pl.pallas_call(
        finish_kernel,
        in_specs=[v_spec] * 9,
        out_specs=(h_spec, h_spec, v_spec),
        out_shape=(
            jax.ShapeDtypeStruct((ff, depth), bf16),
            jax.ShapeDtypeStruct((ff, half), bf16),
            jax.ShapeDtypeStruct((nq // 2, EXAMPLES), f32),
        ),
        scratch_shapes=[
            vm((PIECES - EARLY, ff, width), bf16),
            vm((ff, half), bf16),
            dma((PIECES,)),
            dma((4,)),
        ],
        compiler_params=pltpu.CompilerParams(vmem_limit_bytes=11 << 20),
    )(*held)
    return (gh.T, wg, scores)


def fits(mesh, shapes):
    n = mesh.shape["row"]
    if mesh.shape["col"] != 2 or n % 2 or not 6 <= n <= 16 or PIECES < n // 2 + 4:
        return False
    grad_out, hidden_act, _, proj_in, _, queries, _ = shapes
    parts = mesh.shape["grp"]
    rows_of = grad_out[0] // (parts * n)
    ff = hidden_act[1] // n
    rank = proj_in[1]
    return (
        2 * rows_of == 128
        and grad_out[1] % (2 * PIECES * 256) == 0
        and ff % 64 == 0
        and rank % 32 == 0
        and queries[0] % (16 * n) == 0
        and queries[1] == rank * rank
        and ff * (rows_of * n + grad_out[1]) < 24 << 20
    )


def solution(mesh):
    def run(*args):
        body = fused_body if fits(mesh, [a.shape for a in args]) else plain_body
        return jax.shard_map(
            body,
            mesh=mesh,
            in_specs=(
                P(("grp", "row"), "col"),
                P(("grp", "col"), "row"),
                P("row", "col"),
                P("row", None),
                P("col", None),
                P("row", "col"),
                P(("grp", "row")),
            ),
            out_specs=(P(("grp", "col"), "row"), P(("grp", "row"), "col"), P(("row", "col"), "grp")),
            check_vma=False,
        )(*args)

    return run
```
